32 devices in a mesh: prow: 4 (over y, core), pcol: 8 (over z, x).
Axes of the slice: x: 2, y: 2, z: 4, core: 2. Of those that a mesh axis runs over, the one named last changes fastest.
Arguments:
- matrix: bfloat16 [4096, 2048], P('prow', 'pcol'), may hold values from -6 to 6
- panel_one: bfloat16 [256, 4096], P('pcol', 'prow'), may hold values from -0.375 to 0.375
- panel_two: bfloat16 [256, 4096], P('pcol', 'prow'), may hold values from -0.375 to 0.375
- pivots_one: int32 [256], replicated, may hold values from 0 to 4095, as said below
- pivots_two: int32 [256], replicated, may hold values from 256 to 4095, as said below
Outputs:
- trailing: bfloat16 [4096, 2048], P('prow', 'pcol')
The draws below stay inside these ranges and needn't reach their ends.
Inputs may be any that keep to these rules, and one draw needn't show every extreme that they name: Each pivots_one[i] is either i or a logical row from 256 to 4095; no row is named twice; 4095 is always named. Each pivots_two[i] is either 256 + i or a logical row from 512 to 4095; no row is named twice; 4095 is always named.
All inputs are finite; a program needn't handle non-finite values.
Results may differ from the reference program's by a relative error of at most 0.006.
Values may be sent and summed in bfloat16 or wider, within the bound.
A program may use at most 64 MiB of HBM per device.

```python
import jax
import jax.numpy as jnp
from jax import lax

PANEL = 256
ROWS_DEV = 1024
PROWS = 4
ROWS = 4096
COLS = 2048


def choose_pivots(key, first_row):
    span_rows = ROWS - first_row - PANEL
    shuffled = jax.random.permutation(jax.random.fold_in(key, 31), span_rows - 1)[:PANEL]
    forced = jax.random.randint(jax.random.fold_in(key, 32), (), 0, PANEL)
    position = jnp.arange(PANEL, dtype=jnp.int32)
    shuffled = jnp.where(position == forced, span_rows - 1, shuffled)
    unmoved = (jax.random.randint(jax.random.fold_in(key, 33), (PANEL,), 0, 8) == 0) & (position != forced)
    return jnp.where(unmoved, first_row + position, first_row + PANEL + shuffled).astype(jnp.int32)


def panel_values(key):
    values = jnp.clip(jax.random.normal(key, (PANEL, ROWS), jnp.float32) * 0.0625, -0.375, 0.375)
    return values.astype(jnp.bfloat16)


def draw_panel_one(key, part):
    return panel_values(jax.random.fold_in(key, 11))


def draw_panel_two(key, part):
    return panel_values(jax.random.fold_in(key, 12))


def draw_pivots_one(key, part):
    return choose_pivots(jax.random.fold_in(key, 21), 0)


def draw_pivots_two(key, part):
    return choose_pivots(jax.random.fold_in(key, 22), PANEL)


def levels(own_key, dims, pieces, smallest, high):
    level, own = 1.0, jax.random.fold_in(own_key, 6)
    for axis_at, parts in pieces:
        steps = jnp.exp(jax.random.uniform(jax.random.fold_in(own, axis_at), (parts,), jnp.float32, smallest / len(pieces), high / len(pieces)))
        level = level * jnp.repeat(steps, dims[axis_at] // parts).reshape([-1 if axis == axis_at else 1 for axis in range(len(dims))])
    return level


def normal_values(own_key, shape, deviation, bound, cuts=(), kind=jnp.bfloat16):
    drawn = deviation * jax.random.normal(own_key, shape, jnp.float32)
    if cuts:
        drawn = drawn * levels(own_key, shape, cuts, -0.22, 0.18)
    return jnp.clip(drawn, -bound, bound).astype(kind)


def setup_inputs(seed: int = 0) -> dict:
    key_list = jax.random.split(jax.random.key(seed), 6)
    return {
        "matrix": normal_values(key_list[0], (ROWS, COLS), 1.0, 6.0, ((0, 4), (1, 8))),
        "panel_one": draw_panel_one(jax.random.fold_in(key_list[5], 71), 0),
        "panel_two": draw_panel_two(jax.random.fold_in(key_list[5], 71), 0),
        "pivots_one": draw_pivots_one(jax.random.fold_in(key_list[5], 71), 0),
        "pivots_two": draw_pivots_two(jax.random.fold_in(key_list[5], 71), 0),
    }


def stored_rows(logical):
    block_index = logical // PANEL
    return (block_index % PROWS) * ROWS_DEV + (block_index // PROWS) * PANEL + logical % PANEL


def unit_inverse(strict):
    extent = strict.shape[0]
    identity = jnp.eye(extent, dtype=jnp.float32)
    result = identity - strict
    powered = strict
    for repeat in range((extent - 1).bit_length() - 1):
        powered = jnp.dot(powered, powered, precision=lax.Precision.HIGHEST)
        result = jnp.dot(result, identity + powered, precision=lax.Precision.HIGHEST)
    return result


def reference(matrix, panel_one, panel_two, pivots_one, pivots_two):
    stored = jnp.arange(ROWS, dtype=jnp.int32)
    holder_row = stored // ROWS_DEV
    local_row = stored % ROWS_DEV
    logical = ((local_row // PANEL) * PROWS + holder_row) * PANEL + local_row % PANEL
    current = matrix
    sections = ((panel_one, pivots_one), (panel_two, pivots_two))
    for step_index in range(2):
        panel_now, pivots = sections[step_index]
        first_row = step_index * PANEL
        pivot_at = stored_rows(first_row + jnp.arange(PANEL, dtype=jnp.int32))
        chosen_at = stored_rows(pivots.astype(jnp.int32))
        leaving = current[pivot_at]
        arriving = current[chosen_at]
        current = current.at[chosen_at].set(leaving).at[pivot_at].set(arriving)
        pivot_rows = current[pivot_at].astype(jnp.float32)
        strict = jnp.tril(panel_now[:, pivot_at].T.astype(jnp.float32), -1)
        solved = jnp.dot(unit_inverse(strict), pivot_rows, precision=lax.Precision.HIGHEST).astype(jnp.bfloat16)

        def update_slab(operands, solved=solved, first_row=first_row):
            row_slab, panel_slab, logical_slab = operands
            product = jnp.dot(panel_slab.T.astype(jnp.float32), solved.astype(jnp.float32), precision=lax.Precision.HIGHEST)
            updated = (row_slab.astype(jnp.float32) - product).astype(jnp.bfloat16)
            pivot_part = jnp.take(solved, jnp.clip(logical_slab - first_row, 0, PANEL - 1), axis=0)
            beyond = logical_slab >= first_row + PANEL
            in_block = (logical_slab >= first_row) & (logical_slab < first_row + PANEL)
            return jnp.where(beyond[:, None], updated, jnp.where(in_block[:, None], pivot_part, row_slab))

        slabs = (current.reshape(PROWS, ROWS_DEV, COLS), panel_now.reshape(PANEL, PROWS, ROWS_DEV).transpose(1, 0, 2), logical.reshape(PROWS, ROWS_DEV))
        current = lax.map(update_slab, slabs).reshape(ROWS, COLS)
    return current
```

```python
import functools

import jax
import jax.numpy as jnp
from jax import lax
from jax.experimental import pallas as pl
from jax.experimental.pallas import tpu as pltpu
from jax.sharding import PartitionSpec as P

F32 = jnp.float32
BF16 = jnp.bfloat16
ROW_ROW = (((0,), (0,)), ((), ()))
HEAD_ONE, HEAD_TWO, CHOSEN_ONE, TAIL_ONE, TAIL_TWO = range(5)
LEAD_ONE, LEAD_TWO, CROSS, SOLVED_ONE, SOLVED_TWO, LEAVING_TWO = range(6)


def dot(a, b):
    return jnp.dot(a, b, preferred_element_type=F32)


def dot_t(a, b):
    return lax.dot_general(a, b, ROW_ROW, preferred_element_type=F32)


def halves(a):
    high = a.astype(BF16)
    return high, (a - high.astype(F32)).astype(BF16)


def dot_split(a, b):
    a_high, a_low = halves(a)
    b_high, b_low = halves(b)
    return dot(a_high, b_high) + (dot(a_high, b_low) + dot(a_low, b_high))


def unit_inverse(panel, hooks):
    hooks = list(hooks)

    def pause():
        if hooks:
            hooks.pop(0)()

    extent = panel.shape[0]
    part = extent // 2
    full = panel.astype(F32).T
    row = lax.broadcasted_iota(jnp.int32, (part, extent), 0)
    col = lax.broadcasted_iota(jnp.int32, (part, extent), 1) % part
    strict = jnp.where(row > col, jnp.concatenate([full[:part, :part], full[part:, part:]], axis=1), 0.0)
    zero = jnp.zeros((part, part), F32)

    def diagonal(a):
        left = jnp.concatenate([a[:, :part], zero.astype(a.dtype)], axis=0)
        right = jnp.concatenate([zero.astype(a.dtype), a[:, part:]], axis=0)
        return jnp.concatenate([left, right], axis=1)

    exact = strict.astype(BF16)
    power = dot(exact, diagonal(exact))
    result = jnp.where(row == col, 1.0, 0.0) - strict
    repeats = (part - 1).bit_length() - 1
    for repeat in range(repeats):
        pause()
        if repeat == repeats - 1:
            result = result + dot_split(result, diagonal(power))
        else:
            both = dot_split(jnp.concatenate([result, power], axis=0), diagonal(power))
            result, power = result + both[:part], both[part:]
    upper, lower = result[:, :part], result[:, part:]
    high, low = halves(upper)
    below = full[part:, :part].astype(BF16)
    corner = -dot_split(lower, dot(below, high) + dot(below, low))
    while hooks:
        pause()
    return jnp.concatenate(
        [jnp.concatenate([upper, zero], axis=1), jnp.concatenate([corner, lower], axis=1)], axis=0
    )


def onehot(a, b):
    return (a == b).astype(F32)


def body(
    process_rows, process_cols,
    matrix_hbm, one_hbm, two_hbm, piv_one_hbm, piv_two_hbm, out,
    piv_one, piv_two, matrix, picks, head, tail, sent_sel, sel_in,
    rows_part, pair_rows, group_rows, lead, cross, solved, leaving, inverse,
    l_sem, g_send, g_recv, s_send, s_recv, p_send, p_recv, q_send, q_recv, i_send, i_recv,
):
    width = piv_one.shape[1]
    rows_dev, cols = matrix.shape
    shard = one_hbm.shape[0]
    size_z = process_cols // 2
    groups = process_rows // 2
    my_row = lax.axis_index("prow")
    my_col = lax.axis_index("pcol")
    my_z, my_x = my_col // 2, my_col % 2
    x_peer = my_z * 2 + (1 - my_x)
    group, core = my_row // 2, my_row % 2
    pair = group * 2 + (1 - core)
    mesh_ids = pl.DeviceIdType.MESH
    first, rest = pl.ds(0, width), pl.ds(width, rows_dev - width)
    top, lower_rows = group == 0, group > 0
    lower_zero, lower_one = lower_rows & (core == 0), lower_rows & (core == 1)
    is_zero, is_one = my_row == 0, my_row == 1
    not_zero, not_one = my_row != 0, my_row != 1

    def row_peer(step):
        return lax.rem(my_row + step, process_rows)

    def col_peer(step):
        return lax.rem(my_col + step, process_cols)

    def group_peer(step):
        return lax.rem(group + step, groups) * 2 + core

    def z_peer(step):
        return lax.rem(my_z + step, size_z) * 2 + my_x

    def z_across(step):
        return lax.rem(my_z + step, size_z) * 2 + (1 - my_x)

    cols_at = [col_peer(step) for step in range(process_cols)]
    zs_at = [z_peer(step) for step in range(size_z)]
    groups_at = [group_peer(step) for step in range(groups)]

    barrier = pltpu.get_barrier_semaphore()
    for step in range(1, process_rows):
        pl.semaphore_signal(barrier, 1, device_id={"prow": row_peer(step)}, device_id_type=mesh_ids)
    for step in range(1, process_cols):
        pl.semaphore_signal(barrier, 1, device_id={"pcol": col_peer(step)}, device_id_type=mesh_ids)

    loads = [
        pltpu.make_async_copy(piv_one_hbm, piv_one, l_sem.at[0]),
        pltpu.make_async_copy(piv_two_hbm, piv_two, l_sem.at[1]),
        pltpu.make_async_copy(one_hbm.at[:, first], head.at[0, my_col], l_sem.at[2]),
        pltpu.make_async_copy(one_hbm.at[:, rest], tail.at[0, my_col], l_sem.at[3]),
        pltpu.make_async_copy(matrix_hbm, matrix, l_sem.at[4]),
        pltpu.make_async_copy(two_hbm.at[:, first], head.at[1, my_col], l_sem.at[5]),
        pltpu.make_async_copy(two_hbm.at[:, rest], tail.at[1, my_col], l_sem.at[6]),
    ]
    for load in loads:
        load.start()

    sent = []

    def remote(src, dst, send, recv, device):
        return pltpu.make_async_remote_copy(
            src_ref=src, dst_ref=dst, send_sem=send, recv_sem=recv,
            device_id=device, device_id_type=mesh_ids,
        )

    def push(condition, *makes):
        for make in makes:
            make().start()
            sent.append((condition, make))

    def slot_of(piece, col):
        return head.at[piece, col] if piece < 3 else tail.at[piece - 3, col]

    def source_of(piece):
        if piece == CHOSEN_ONE:
            return head.at[piece, my_col]
        panel = (one_hbm, two_hbm, None, one_hbm, two_hbm)[piece]
        return panel.at[:, first if piece < 3 else rest]

    def gather_copy(piece, index, col):
        return lambda: remote(
            source_of(piece), slot_of(piece, my_col), g_send.at[piece, index], g_recv.at[piece, my_col], {"pcol": col}
        )

    def forward_copy(piece, step):
        return lambda: remote(
            slot_of(piece, zs_at[step]), slot_of(piece, zs_at[step]), g_send.at[piece, size_z + step],
            g_recv.at[piece, zs_at[step]], {"pcol": x_peer},
        )

    def send_all(piece, condition):
        push(condition, *[gather_copy(piece, step, cols_at[step]) for step in range(1, process_cols)])

    def send_x(piece, condition):
        push(condition, gather_copy(piece, 0, x_peer))

    def send_z(piece, condition):
        push(condition, *[gather_copy(piece, step, zs_at[step]) for step in reversed(range(1, size_z))])

    def arrive(piece, col):
        slot = slot_of(piece, col)
        remote(slot, slot, g_send.at[piece, 0], g_recv.at[piece, col], {"pcol": x_peer}).wait_recv()

    def forward(piece, step, condition):
        arrive(piece, z_peer(step))
        push(condition, forward_copy(piece, step))

    def take_x(piece):
        for step in range(size_z):
            arrive(piece, z_across(step))

    def flat(block):
        return block.reshape(process_cols * shard, block.shape[-1])

    def item_place(item):
        return {
            LEAD_ONE: lead.at[0], LEAD_TWO: lead.at[1], CROSS: cross,
            SOLVED_ONE: solved.at[0], SOLVED_TWO: solved.at[1], LEAVING_TWO: leaving,
        }[item]

    def item_copy(item, step, source=None):
        def make():
            place = item_place(item)
            device = {"prow": groups_at[step] if step else pair}
            return remote(source() if source else place, place, i_send.at[item, step], i_recv.at[item], device)

        return make

    def item_down(item, condition, source=None):
        push(condition, *[item_copy(item, step, source) for step in range(1, groups)])

    def item_across(item, condition, source=None):
        push(condition, item_copy(item, 0, source))

    def item_wait(item):
        item_copy(item, 0)().wait_recv()

    def item_relay(item, condition):
        @pl.when(condition)
        def _():
            item_wait(item)
            item_across(item, condition)

    pl.semaphore_wait(barrier, process_rows - 1 + process_cols - 1)

    @pl.when(is_zero)
    def _():
        send_all(HEAD_ONE, is_zero)
        item_across(LEAD_ONE, is_zero, lambda: matrix_hbm.at[first, :])
        item_down(LEAD_ONE, is_zero, lambda: matrix_hbm.at[first, :])

    @pl.when(is_one)
    def _():
        send_all(HEAD_TWO, is_one)

    @pl.when(not_zero)
    def _():
        send_x(HEAD_ONE, not_zero)
        send_z(HEAD_ONE, not_zero)

    send_x(TAIL_ONE, None)
    send_z(TAIL_ONE, None)

    @pl.when(lower_rows)
    def _():
        send_x(HEAD_TWO, lower_rows)
        send_z(HEAD_TWO, lower_rows)

    send_x(TAIL_TWO, None)

    @pl.when(lower_rows)
    def _():
        send_z(TAIL_TWO, lower_rows)

    local = lax.broadcasted_iota(jnp.int32, (rows_dev, width), 0)
    logical = (local // width * process_rows + my_row) * width + local % width
    for load in loads[:4]:
        load.wait()
    hit_one, hit_two = onehot(logical, piv_one[...]), onehot(logical, piv_two[...])
    picks[0], picks[1] = hit_one.astype(BF16), hit_two.astype(BF16)
    sent_sel[...] = (dot(head[0, my_col], picks[1, first, :]) + dot(tail[0, my_col], picks[1, rest, :])).astype(BF16)

    def sel_copy():
        return remote(sent_sel, sel_in.at[my_row], s_send, s_recv.at[my_row], {"prow": 1})

    @pl.when(not_one)
    def _():
        push(not_one, sel_copy)

    loads[4].wait()
    rows_part[1 - core] = dot_t(picks[1 - core], matrix[...]).astype(BF16)

    def pair_copy():
        return remote(rows_part.at[1 - core], pair_rows, p_send, p_recv, {"prow": pair})

    push(None, pair_copy)
    rows_part[core] = dot_t(picks[core], matrix[...]).astype(BF16)
    for load in loads[5:]:
        load.wait()

    @pl.when(is_one)
    def _():
        selected = sent_sel[...].astype(F32)
        for step in range(1, process_rows):
            source = row_peer(step)
            slot = sel_in.at[source]
            remote(slot, slot, s_send, s_recv.at[source], {"prow": source}).wait_recv()
            selected = selected + sel_in[source].astype(F32)
        head[2, my_col] = selected.astype(BF16)
        send_all(CHOSEN_ONE, is_one)

    @pl.when(top)
    def _():
        send_z(TAIL_TWO, top)

    keep_one = 1.0 - jnp.sum(hit_one, axis=1, keepdims=True)
    keep_two = 1.0 - jnp.sum(hit_two, axis=1, keepdims=True)

    @pl.when(is_zero)
    def _():
        lead[0] = matrix[first, :]

    @pl.when(is_one)
    def _():
        item_wait(LEAD_ONE)
        swapped = matrix[first, :].astype(F32) * keep_one[:width] + dot(picks[0, first, :], lead[0])
        lead[1] = swapped.astype(BF16)
        item_down(LEAD_TWO, is_one)

    remote(pair_rows, pair_rows, p_send, p_recv, {"prow": pair}).wait_recv()
    rows_part[core] = (rows_part[core].astype(F32) + pair_rows[...].astype(F32)).astype(BF16)

    def group_copy():
        return remote(rows_part.at[core], group_rows.at[group], q_send, q_recv.at[group], {"prow": core})

    @pl.when(lower_rows)
    def _():
        push(lower_rows, group_copy)
        for piece in (HEAD_ONE, TAIL_ONE):
            for step in range(1, size_z):
                forward(piece, step, lower_rows)

        item_relay(LEAD_ONE, lower_zero)
        item_relay(LEAD_TWO, lower_one)
        for step in range(1, size_z):
            forward(HEAD_TWO, step, lower_rows)
        item_relay(CROSS, lower_one)
        for step in range(1, size_z):
            forward(TAIL_TWO, step, lower_rows)
        item_relay(SOLVED_ONE, lower_zero)
        item_relay(SOLVED_TWO, lower_one)

    @pl.when(top)
    def _():
        for step in range(1, process_cols):
            col = col_peer(step)
            slot = head.at[core, col]
            remote(slot, slot, g_send.at[0, 0], g_recv.at[core, col], {"pcol": x_peer}).wait_recv()

        def hook(step):
            def run():
                @pl.when(is_one)
                def _():
                    forward(HEAD_ONE, step, is_one)
                forward(TAIL_ONE, step, top)
            return run

        result = unit_inverse(flat(head[core]), [hook(step) for step in range(1, size_z)])
        inverse[0], inverse[1] = halves(result)

    def solve(incoming):
        return (dot(inverse[0], incoming) + dot(inverse[1], incoming)).astype(BF16)

    def chosen():
        total = rows_part[core].astype(F32)
        for source in range(1, groups):
            slot = group_rows.at[source]
            remote(slot, slot, q_send, q_recv.at[source], {"prow": pair}).wait_recv()
            total = total + group_rows[source].astype(F32)
        return total.astype(BF16)

    @pl.when(is_zero)
    def _():
        solved[0] = solve(chosen())
        item_across(SOLVED_ONE, is_zero)
        item_down(SOLVED_ONE, is_zero)

    @pl.when(is_one)
    def _():
        second = chosen()
        take_x(HEAD_ONE)
        item_down(CROSS, is_one, lambda: head.at[0])
        for step in range(1, process_cols):
            arrive(CHOSEN_ONE, col_peer(step))
        first_across = jnp.broadcast_to(piv_one[...], (width, width))
        second_down = jnp.broadcast_to(piv_two[...].astype(F32), (width, width)).T.astype(jnp.int32)
        match = onehot(second_down, first_across)
        moved = jnp.sum(match, axis=1, keepdims=True)
        swapped = second.astype(F32) * (1.0 - moved) + dot(match.astype(BF16), lead[0])
        item_wait(SOLVED_ONE)
        incoming = (swapped - dot_t(flat(head[2]), solved[0])).astype(BF16)
        solved[1] = solve(incoming)
        item_across(SOLVED_TWO, is_one)
        item_down(SOLVED_TWO, is_one)
        leaving[...] = (lead[1].astype(F32) - dot_t(flat(head[0]), solved[0])).astype(BF16)
        item_across(LEAVING_TWO, is_one)

    @pl.when(top)
    def _():
        for step in range(1, size_z):
            forward(TAIL_TWO, step, top)

    @pl.when(lower_one)
    def _():
        item_wait(LEAD_ONE)

    @pl.when(lower_zero)
    def _():
        item_wait(LEAD_TWO)
        item_wait(CROSS)

    matrix[...] = (matrix[...].astype(F32) * keep_one + dot(picks[0], lead[0])).astype(BF16)
    take_x(TAIL_ONE)

    @pl.when(lower_one)
    def _():
        item_wait(SOLVED_ONE)

    matrix[rest, :] = (matrix[rest, :].astype(F32) - dot_t(flat(tail[0]), solved[0])).astype(BF16)

    @pl.when(lower_rows)
    def _():
        leaving[...] = (lead[1].astype(F32) - dot_t(flat(cross[...]), solved[0])).astype(BF16)
        take_x(HEAD_ONE)
        matrix[first, :] = (matrix[first, :].astype(F32) - dot_t(flat(head[0]), solved[0])).astype(BF16)

    @pl.when(is_zero)
    def _():
        item_wait(LEAVING_TWO)

    matrix[...] = (matrix[...].astype(F32) * keep_two + dot(picks[1], leaving[...])).astype(BF16)

    @pl.when(core == 0)
    def _():
        item_wait(SOLVED_TWO)

    @pl.when(lower_rows)
    def _():
        take_x(HEAD_TWO)
        out[first, :] = (matrix[first, :].astype(F32) - dot_t(flat(head[1]), solved[1])).astype(BF16)

    @pl.when(top)
    def _():
        out[first, :] = solved[core]

    take_x(TAIL_TWO)
    out[rest, :] = (matrix[rest, :].astype(F32) - dot_t(flat(tail[1]), solved[1])).astype(BF16)

    for condition, make in sent:
        if condition is None:
            make().wait_send()
        else:
            pl.when(condition)(lambda make=make: make().wait_send())


def on_device(matrix, panel_one, panel_two, pivots_one, pivots_two):
    process_rows = lax.axis_size("prow")
    process_cols = lax.axis_size("pcol")
    shard, rows_dev = panel_one.shape
    width = pivots_one.shape[0]
    cols = matrix.shape[1]
    vmem = pl.BlockSpec(memory_space=pltpu.VMEM)
    hbm = pl.BlockSpec(memory_space=pltpu.HBM)
    dma = pltpu.SemaphoreType.DMA
    assert rows_dev > width and shard * process_cols == width
    assert process_cols % 2 == 0 and process_rows % 2 == 0
    groups = process_rows // 2
    return pl.pallas_call(
        functools.partial(body, process_rows, process_cols),
        out_shape=jax.ShapeDtypeStruct(matrix.shape, BF16),
        in_specs=[hbm] * 5,
        out_specs=vmem,
        scratch_shapes=[
            pltpu.VMEM((1, width), jnp.int32),
            pltpu.VMEM((1, width), jnp.int32),
            pltpu.VMEM((rows_dev, cols), BF16),
            pltpu.VMEM((2, rows_dev, width), BF16),
            pltpu.VMEM((3, process_cols, shard, width), BF16),
            pltpu.VMEM((2, process_cols, shard, rows_dev - width), BF16),
            pltpu.VMEM((shard, width), BF16),
            pltpu.VMEM((process_rows, shard, width), BF16),
            pltpu.VMEM((2, width, cols), BF16),
            pltpu.VMEM((width, cols), BF16),
            pltpu.VMEM((groups, width, cols), BF16),
            pltpu.VMEM((2, width, cols), BF16),
            pltpu.VMEM((process_cols, shard, width), BF16),
            pltpu.VMEM((2, width, cols), BF16),
            pltpu.VMEM((width, cols), BF16),
            pltpu.VMEM((2, width, width), BF16),
            dma((7,)),
            dma((5, process_cols)), dma((5, process_cols)),
            dma, dma((process_rows,)),
            dma, dma,
            dma, dma((groups,)),
            dma((6, groups)), dma((6,)),
        ],
        compiler_params=pltpu.CompilerParams(
            collective_id=0, has_side_effects=True, vmem_limit_bytes=32 * 1024 * 1024
        ),
    )(*[pltpu.with_memory_space_constraint(a, pltpu.HBM) for a in (matrix, panel_one, panel_two, pivots_one.reshape(1, width), pivots_two.reshape(1, width))])


def solution(mesh):
    placed = (P("prow", "pcol"), P("pcol", "prow"), P("pcol", "prow"), P(), P())
    return jax.shard_map(
        on_device, mesh=mesh, in_specs=placed, out_specs=P("prow", "pcol"), check_vma=False
    )
```

```python
import functools

import jax
import jax.numpy as jnp
from jax import lax
from jax.experimental import pallas as pl
from jax.experimental.pallas import tpu as pltpu
from jax.sharding import PartitionSpec as P

F32 = jnp.float32
BF16 = jnp.bfloat16
ROW_ROW = (((0,), (0,)), ((), ()))
LEAD_ONE, LEAD_TWO, CROSS, SOLVED_ONE, SOLVED_TWO, LEAVING_TWO = range(6)


def dot(a, b):
    return jnp.dot(a, b, preferred_element_type=F32)


def dot_t(a, b):
    return lax.dot_general(a, b, ROW_ROW, preferred_element_type=F32)


def halves(a):
    high = a.astype(BF16)
    return high, (a - high.astype(F32)).astype(BF16)


def dot_split(a, b):
    a_high, a_low = halves(a)
    b_high, b_low = halves(b)
    return dot(a_high, b_high) + (dot(a_high, b_low) + dot(a_low, b_high))


def dot_short(a, b):
    return dot(a.astype(BF16), b.astype(BF16))


def unit_inverse(panel, pause):
    extent = panel.shape[0]
    part = extent // 2
    full = panel.astype(F32).T
    row = lax.broadcasted_iota(jnp.int32, (part, extent), 0)
    col = lax.broadcasted_iota(jnp.int32, (part, extent), 1) % part
    strict = jnp.where(row > col, jnp.concatenate([full[:part, :part], full[part:, part:]], axis=1), 0.0)
    zero = jnp.zeros((part, part), F32)

    def diagonal(a):
        left = jnp.concatenate([a[:, :part], zero.astype(a.dtype)], axis=0)
        right = jnp.concatenate([zero.astype(a.dtype), a[:, part:]], axis=0)
        return jnp.concatenate([left, right], axis=1)

    exact = strict.astype(BF16)
    power = dot(exact, diagonal(exact))
    result = jnp.where(row == col, 1.0, 0.0) - strict
    repeats = (part - 1).bit_length() - 1
    for repeat in range(repeats):
        pause(repeat)
        multiply = dot_split if repeat < 2 else dot_short
        if repeat == repeats - 1:
            result = result + multiply(result, diagonal(power))
        else:
            both = multiply(jnp.concatenate([result, power], axis=0), diagonal(power))
            result, power = result + both[:part], both[part:]
    upper, lower = result[:, :part], result[:, part:]
    high, low = halves(upper)
    below = full[part:, :part].astype(BF16)
    corner = -dot_split(lower, dot(below, high) + dot(below, low))
    return jnp.concatenate(
        [jnp.concatenate([upper, zero], axis=1), jnp.concatenate([corner, lower], axis=1)], axis=0
    )


def onehot(a, b):
    return (a == b).astype(F32)


def body(
    process_rows, process_cols,
    matrix_hbm, one_hbm, two_hbm, piv_one_hbm, piv_two_hbm, out,
    piv_one, piv_two, matrix, picks, panels, chosen_panel, sent_sel, sel_in,
    rows_part, pair_rows, group_rows, lead, cross, solved, leaving, inverse,
    l_sem, g_send, z_recv, f_recv, x_recv, d_send, d_recv, s_send, s_recv,
    p_send, p_recv, q_send, q_recv, i_send, i_recv,
):
    width = piv_one.shape[1]
    rows_dev, cols = matrix.shape
    shard = one_hbm.shape[0]
    half = width // 2
    blocks = rows_dev // width
    size_z = process_cols // 2
    groups = process_rows // 2
    my_row = lax.axis_index("prow")
    my_col = lax.axis_index("pcol")
    my_z, my_x = my_col // 2, my_col % 2
    x_peer = my_z * 2 + (1 - my_x)
    group, core = my_row // 2, my_row % 2
    pair = group * 2 + (1 - core)
    mesh_ids = pl.DeviceIdType.MESH
    panel_hbm = (one_hbm, two_hbm)
    span = [pl.ds(block * width, width) for block in range(blocks)]
    whole, rest = pl.ds(0, rows_dev), pl.ds(width, rows_dev - width)
    top, lower = group == 0, group > 0
    is_zero, is_one, not_one = my_row == 0, my_row == 1, my_row != 1
    lower_zero, lower_one = lower & (core == 0), lower & (core == 1)

    def row_peer(step):
        return lax.rem(my_row + step, process_rows)

    cols_at = [lax.rem(my_col + step, process_cols) for step in range(process_cols)]
    zs_at = [lax.rem(my_z + step, size_z) * 2 + my_x for step in range(size_z)]
    across_at = [lax.rem(my_z + step, size_z) * 2 + (1 - my_x) for step in range(size_z)]
    groups_at = [lax.rem(group + step, groups) * 2 + core for step in range(groups)]
    odd = my_z % 2
    beside = (my_z + 1 - 2 * odd) * 2 + my_x
    at_end = (my_z == 0) | (my_z == size_z - 1)
    by_start, by_end = my_z == 1, my_z == size_z - 2
    near_end = by_start | by_end
    far_start, far_end = my_x, (size_z - 1) * 2 + my_x

    barrier = pltpu.get_barrier_semaphore()
    for step in range(1, process_rows):
        pl.semaphore_signal(barrier, 1, device_id={"prow": row_peer(step)}, device_id_type=mesh_ids)
    for step in range(1, process_cols):
        pl.semaphore_signal(barrier, 1, device_id={"pcol": cols_at[step]}, device_id_type=mesh_ids)

    loads = [
        pltpu.make_async_copy(piv_one_hbm, piv_one, l_sem.at[0]),
        pltpu.make_async_copy(piv_two_hbm, piv_two, l_sem.at[1]),
        pltpu.make_async_copy(one_hbm, panels.at[0, my_col], l_sem.at[2]),
        pltpu.make_async_copy(matrix_hbm, matrix, l_sem.at[3]),
        pltpu.make_async_copy(two_hbm, panels.at[1, my_col], l_sem.at[4]),
    ]
    for load in loads:
        load.start()

    def remote(src, dst, send, recv, device):
        return pltpu.make_async_remote_copy(
            src_ref=src, dst_ref=dst, send_sem=send, recv_sem=recv,
            device_id=device, device_id_type=mesh_ids,
        )

    def arrived(ref, recv):
        remote(ref, ref, g_send, recv, {"pcol": x_peer}).wait_recv()

    def departed(ref, send):
        remote(ref, ref, send, x_recv.at[0], {"pcol": x_peer}).wait_send()

    def place(panel, block, col):
        return panels.at[panel, col, :, span[block]]

    def several(panel, block, count):
        return panels.at[panel, pl.ds(0, count), :, span[block]]

    def along(panel, block, source, col, target):
        remote(
            source, place(panel, block, col), g_send, z_recv.at[panel, block], {"pcol": target}
        ).start()

    def send_z(panel, block):
        for step in reversed(range(1, size_z)):
            across_ends = at_end & ((zs_at[step] // 2 == 0) | (zs_at[step] // 2 == size_z - 1))

            @pl.when(jnp.logical_not(across_ends))
            def _(step=step):
                along(panel, block, panel_hbm[panel].at[:, span[block]], my_col, zs_at[step])

    def send_x(panel, part):
        remote(
            panel_hbm[panel].at[:, part], panels.at[panel, my_col, :, part], g_send, x_recv.at[panel], {"pcol": x_peer}
        ).start()

    def forward(panel, block):
        arrived(several(panel, block, size_z - 1), z_recv.at[panel, block])

        @pl.when(by_end)
        def _():
            along(panel, block, place(panel, block, far_start), far_start, far_end)

        @pl.when(by_start)
        def _():
            along(panel, block, place(panel, block, far_end), far_end, far_start)

        for step in range(1, size_z - panel):
            col = lax.rem(my_z + step + panel * (1 - odd), size_z) * 2 + my_x
            slot = place(panel, block, col)
            remote(slot, slot, g_send, f_recv.at[panel, block], {"pcol": x_peer}).start()

    def take(panel, block):
        arrived(several(panel, block, size_z - 1 - panel), f_recv.at[panel, block])

    def take_x(panel, part):
        arrived(panels.at[panel, x_peer, :, part], x_recv.at[panel])

    def pass_beside(part):
        take_x(1, part)
        slot = panels.at[1, x_peer, :, part]
        remote(slot, slot, g_send, x_recv.at[2], {"pcol": beside}).start()

    def take_beside(part):
        arrived(panels.at[1, x_peer, :, part], x_recv.at[2])

    def all_departed(part):
        @pl.when(at_end)
        def _():
            departed(panels.at[:, pl.ds(0, process_cols - 2), :, part], g_send)

        @pl.when(near_end)
        def _():
            departed(panels.at[:, :, :, part], g_send)

        @pl.when(jnp.logical_not(at_end | near_end))
        def _():
            departed(panels.at[:, pl.ds(0, process_cols - 1), :, part], g_send)

    def direct(index, source, target):
        for step in range(1, process_cols):
            remote(source, target, d_send.at[index], d_recv.at[index], {"pcol": cols_at[step]}).start()

    def others():
        return panels.at[0, pl.ds(0, process_cols - 1), :, span[0]]

    def take_direct(index):
        arrived(others(), d_recv.at[index])

    def block_of(panel, block):
        return panels[panel, :, :, span[block]].reshape(width, width)

    def item_copy(item, peer, source=None):
        target = (lead.at[0], lead.at[1], cross, solved.at[0], solved.at[1], leaving)[item]
        return remote(
            target if source is None else source, target, i_send.at[item], i_recv.at[item], {"prow": peer}
        )

    def item_down(item, source=None):
        for step in range(1, groups):
            item_copy(item, groups_at[step], source).start()

    def item_across(item, source=None):
        item_copy(item, pair, source).start()

    def item_wait(item):
        item_copy(item, pair).wait_recv()

    def item_relay(item):
        item_wait(item)
        item_across(item)

    def item_sent(item, copies):
        departed(group_rows.at[pl.ds(0, copies)], i_send.at[item])

    pl.semaphore_wait(barrier, process_rows - 1 + process_cols - 1)

    @pl.when(is_zero)
    def _():
        direct(0, one_hbm.at[:, span[0]], place(0, 0, my_col))
        item_across(LEAD_ONE, matrix_hbm.at[span[0], :])
        item_down(LEAD_ONE, matrix_hbm.at[span[0], :])

    @pl.when(is_one)
    def _():
        direct(1, two_hbm.at[:, span[0]], place(1, 0, my_col))
        send_x(0, rest)

    @pl.when(is_zero)
    def _():
        send_x(0, rest)
        for block in range(1, blocks):
            send_z(0, block)

    @pl.when(lower)
    def _():
        for panel in range(2):
            send_x(panel, whole)
        for block in range(blocks):
            send_z(0, block)

    for load in loads[:3]:
        load.wait()
    local = lax.broadcasted_iota(jnp.int32, (width, width), 0)
    for block in range(blocks):
        hit = onehot(local, piv_two[...] - (block * process_rows + my_row) * width)
        picks[1, span[block], :] = hit.astype(BF16)
    sent_sel[...] = dot(panels[0, my_col], picks[1]).astype(BF16)

    def sel_copy():
        return remote(sent_sel, sel_in.at[my_row], s_send, s_recv, {"prow": 1})

    @pl.when(not_one)
    def _():
        sel_copy().start()

    for block in range(blocks):
        hit = onehot(local, piv_one[...] - (block * process_rows + my_row) * width)
        picks[0, span[block], :] = hit.astype(BF16)
    loads[3].wait()
    for which in range(2):
        rows_part[which] = dot_t(picks[which], matrix[...]).astype(BF16).reshape(2, half, cols)

    def top_copy():
        return remote(rows_part.at[1 - core], pair_rows, p_send, p_recv, {"prow": pair})

    def half_copy():
        return remote(rows_part.at[:, 1 - core], pair_rows, p_send, p_recv, {"prow": pair})

    def rows_copy(which):
        return remote(
            rows_part.at[which, core], group_rows.at[group, core], q_send, q_recv, {"prow": which}
        )

    def swap(which, rows):
        pick = picks[which]
        kept = 1.0 - jnp.sum(pick.astype(F32), axis=1, keepdims=True)
        matrix[...] = (matrix[...].astype(F32) * kept + dot(pick, rows)).astype(BF16)

    def update(panel, block, to):
        to[span[block], :] = (
            matrix[span[block], :].astype(F32) - dot_t(block_of(panel, block), solved[panel])
        ).astype(BF16)

    def chosen():
        total = rows_part[core].astype(F32) + pair_rows[...].astype(F32)
        arrived(group_rows.at[pl.ds(0, groups - 1)], q_recv)
        for source in range(1, groups):
            total = total + group_rows[source].astype(F32)
        return total.astype(BF16).reshape(width, cols)

    def solve(incoming):
        return (dot(inverse[0], incoming) + dot(inverse[1], incoming)).astype(BF16)

    @pl.when(top)
    def _():
        top_copy().start()

    @pl.when(is_zero)
    def _():
        send_x(1, rest)
        for block in range(1, blocks):
            send_z(1, block)
        lead[0] = matrix[span[0], :]

    @pl.when(is_one)
    def _():
        selected = sent_sel[...].astype(F32)
        arrived(sel_in.at[pl.ds(0, process_rows - 1)], s_recv)
        for step in range(1, process_rows):
            selected = selected + sel_in[row_peer(step)].astype(F32)
        chosen_panel[my_col] = selected.astype(BF16)
        direct(2, chosen_panel.at[my_col], chosen_panel.at[my_col])
        direct(0, one_hbm.at[:, span[0]], place(0, 0, my_col))
        for block in range(1, blocks):
            send_z(0, block)
        send_x(1, rest)
        for block in range(1, blocks):
            send_z(1, block)
        item_wait(LEAD_ONE)
        pick = picks[0, span[0], :]
        kept = 1.0 - jnp.sum(pick.astype(F32), axis=1, keepdims=True)
        lead[1] = (matrix[span[0], :].astype(F32) * kept + dot(pick, lead[0])).astype(BF16)
        item_down(LEAD_TWO)

    @pl.when(top)
    def _():
        loads[4].wait()

    @pl.when(is_zero)
    def _():
        take_direct(0)

        def pause(step):
            if step == 4:
                forward(0, 1)

        result = unit_inverse(block_of(0, 0), pause)
        inverse[0], inverse[1] = halves(result)
        top_copy().wait_recv()
        solved[0] = solve(chosen())
        item_across(SOLVED_ONE)
        item_down(SOLVED_ONE)
        for block in range(2, blocks):
            forward(0, block)

    @pl.when(is_one)
    def _():
        take_direct(1)

        def pause(step):
            pass

        result = unit_inverse(block_of(1, 0), pause)
        inverse[0], inverse[1] = halves(result)
        first_across = jnp.broadcast_to(piv_one[...], (width, width))
        second_down = jnp.broadcast_to(piv_two[...].astype(F32), (width, width)).T.astype(jnp.int32)
        take_direct(0)
        cross[...] = panels[0, :, :, span[0]]
        item_down(CROSS)
        for block in range(1, blocks):
            forward(0, block)
        match = onehot(second_down, first_across)
        kept = 1.0 - jnp.sum(match, axis=1, keepdims=True)
        top_copy().wait_recv()
        swapped = chosen().astype(F32) * kept + dot(match.astype(BF16), lead[0])
        take_direct(2)
        item_wait(SOLVED_ONE)
        incoming = (swapped - dot_t(chosen_panel[...].reshape(width, width), solved[0])).astype(BF16)
        solved[1] = solve(incoming)
        item_down(SOLVED_TWO)
        item_across(SOLVED_TWO)
        leaving[...] = (lead[1].astype(F32) - dot_t(block_of(0, 0), solved[0])).astype(BF16)
        item_across(LEAVING_TWO)

    @pl.when(top)
    def _():
        pass_beside(rest)
        for block in range(1, blocks):
            forward(1, block)
        swap(0, lead[0])
        take_x(0, rest)
        for block in range(1, blocks):
            take(0, block)
            update(0, block, matrix)

    @pl.when(is_zero)
    def _():
        item_wait(LEAVING_TWO)
        swap(1, leaving[...])
        item_wait(SOLVED_TWO)
        out[span[0], :] = solved[0]

    @pl.when(is_one)
    def _():
        swap(1, leaving[...])
        out[span[0], :] = solved[1]

    @pl.when(top)
    def _():
        take_beside(rest)
        for block in range(1, blocks):
            take(1, block)
            update(1, block, out)

    @pl.when(lower)
    def _():
        half_copy().start()
        for block in range(blocks):
            send_z(1, block)
        half_copy().wait_recv()
        for which in range(2):
            rows_part[which, core] = (
                rows_part[which, core].astype(F32) + pair_rows[which].astype(F32)
            ).astype(BF16)
            rows_copy(which).start()
        loads[4].wait()
        forward(0, 0)

    @pl.when(lower_zero)
    def _():
        item_relay(LEAD_ONE)

    @pl.when(lower_one)
    def _():
        item_wait(LEAD_ONE)

    @pl.when(lower)
    def _():
        swap(0, lead[0])
        forward(0, 1)
        pass_beside(whole)
        for block in range(2, blocks):
            forward(0, block)

    @pl.when(lower_one)
    def _():
        item_relay(LEAD_TWO)

    @pl.when(lower)
    def _():
        for block in range(2):
            forward(1, block)

    @pl.when(lower_one)
    def _():
        item_relay(CROSS)

    @pl.when(lower_zero)
    def _():
        item_relay(SOLVED_ONE)

    @pl.when(lower)
    def _():
        for block in range(2, blocks):
            forward(1, block)

    @pl.when(lower_zero)
    def _():
        item_wait(LEAD_TWO)
        item_wait(CROSS)

    @pl.when(lower_one)
    def _():
        item_relay(SOLVED_TWO)
        item_wait(SOLVED_ONE)

    @pl.when(lower)
    def _():
        take_x(0, whole)
        for block in range(blocks):
            take(0, block)
            update(0, block, matrix)
        leaving[...] = (lead[1].astype(F32) - dot_t(cross[...].reshape(width, width), solved[0])).astype(BF16)
        swap(1, leaving[...])

    @pl.when(lower_zero)
    def _():
        item_wait(SOLVED_TWO)

    @pl.when(lower)
    def _():
        take_beside(whole)
        for block in range(blocks):
            take(1, block)
            update(1, block, out)
        all_departed(whole)
        half_copy().wait_send()
        departed(rows_part.at[:, core], q_send)

    @pl.when(lower_zero)
    def _():
        item_sent(LEAD_ONE, 1)
        item_sent(SOLVED_ONE, 1)

    @pl.when(lower_one)
    def _():
        item_sent(LEAD_TWO, 1)
        item_sent(CROSS, 1)
        item_sent(SOLVED_TWO, 1)

    @pl.when(top)
    def _():
        all_departed(rest)
        top_copy().wait_send()
        departed(others(), d_send.at[0])

    @pl.when(is_zero)
    def _():
        item_sent(LEAD_ONE, groups)
        item_sent(SOLVED_ONE, groups)

    @pl.when(is_one)
    def _():
        departed(others(), d_send.at[1])
        departed(others(), d_send.at[2])
        item_sent(LEAD_TWO, groups - 1)
        item_sent(CROSS, groups - 1)
        item_sent(SOLVED_TWO, groups)
        item_sent(LEAVING_TWO, 1)

    @pl.when(not_one)
    def _():
        sel_copy().wait_send()


def on_device(matrix, panel_one, panel_two, pivots_one, pivots_two):
    process_rows = lax.axis_size("prow")
    process_cols = lax.axis_size("pcol")
    shard, rows_dev = panel_one.shape
    width = pivots_one.shape[0]
    cols = matrix.shape[1]
    vmem = pl.BlockSpec(memory_space=pltpu.VMEM)
    hbm = pl.BlockSpec(memory_space=pltpu.HBM)
    dma = pltpu.SemaphoreType.DMA
    assert rows_dev > width and rows_dev % width == 0 and shard * process_cols == width
    assert process_cols % 4 == 0 and process_cols >= 8 and process_rows % 2 == 0
    groups = process_rows // 2
    blocks = rows_dev // width
    operands = (matrix, panel_one, panel_two, pivots_one.reshape(1, width), pivots_two.reshape(1, width))
    return pl.pallas_call(
        functools.partial(body, process_rows, process_cols),
        out_shape=jax.ShapeDtypeStruct(matrix.shape, BF16),
        in_specs=[hbm] * 5,
        out_specs=vmem,
        scratch_shapes=[
            pltpu.VMEM((1, width), jnp.int32),
            pltpu.VMEM((1, width), jnp.int32),
            pltpu.VMEM((rows_dev, cols), BF16),
            pltpu.VMEM((2, rows_dev, width), BF16),
            pltpu.VMEM((2, process_cols, shard, rows_dev), BF16),
            pltpu.VMEM((process_cols, shard, width), BF16),
            pltpu.VMEM((shard, width), BF16),
            pltpu.VMEM((process_rows, shard, width), BF16),
            pltpu.VMEM((2, 2, width // 2, cols), BF16),
            pltpu.VMEM((2, width // 2, cols), BF16),
            pltpu.VMEM((groups, 2, width // 2, cols), BF16),
            pltpu.VMEM((2, width, cols), BF16),
            pltpu.VMEM((process_cols, shard, width), BF16),
            pltpu.VMEM((2, width, cols), BF16),
            pltpu.VMEM((width, cols), BF16),
            pltpu.VMEM((2, width, width), BF16),
            dma((5,)),
            dma, dma((2, blocks)), dma((2, blocks)), dma((3,)),
            dma((3,)), dma((3,)),
            dma, dma,
            dma, dma,
            dma, dma,
            dma((6,)), dma((6,)),
        ],
        compiler_params=pltpu.CompilerParams(
            collective_id=0, has_side_effects=True, vmem_limit_bytes=32 * 1024 * 1024
        ),
    )(*[pltpu.with_memory_space_constraint(operand, pltpu.HBM) for operand in operands])


def solution(mesh):
    placed = (P("prow", "pcol"), P("pcol", "prow"), P("pcol", "prow"), P(), P())
    return jax.shard_map(
        on_device, mesh=mesh, in_specs=placed, out_specs=P("prow", "pcol"), check_vma=False
    )
```

```python
import functools

import jax
import jax.numpy as jnp
from jax import lax
from jax.experimental import pallas as pl
from jax.experimental.pallas import tpu as pltpu
from jax.sharding import PartitionSpec as P

F32 = jnp.float32
BF16 = jnp.bfloat16
ROW_ROW = (((0,), (0,)), ((), ()))
LEAD_ONE, LEAD_TWO, CROSS, SOLVED_ONE, SOLVED_TWO, LEAVING_TWO = range(6)


def dot(a, b):
    return jnp.dot(a, b, preferred_element_type=F32)


def dot_t(a, b):
    return lax.dot_general(a, b, ROW_ROW, preferred_element_type=F32)


def halves(a):
    high = a.astype(BF16)
    return high, (a - high.astype(F32)).astype(BF16)


def dot_split(a, b):
    a_high, a_low = halves(a)
    b_high, b_low = halves(b)
    return dot(a_high, b_high) + (dot(a_high, b_low) + dot(a_low, b_high))


def dot_short(a, b):
    return dot(a.astype(BF16), b.astype(BF16))


def unit_inverse(panel, pause):
    extent = panel.shape[0]
    part = extent // 2
    full = panel.astype(F32).T
    row = lax.broadcasted_iota(jnp.int32, (part, extent), 0)
    col = lax.broadcasted_iota(jnp.int32, (part, extent), 1) % part
    strict = jnp.where(row > col, jnp.concatenate([full[:part, :part], full[part:, part:]], axis=1), 0.0)
    zero = jnp.zeros((part, part), F32)

    def diagonal(a):
        left = jnp.concatenate([a[:, :part], zero.astype(a.dtype)], axis=0)
        right = jnp.concatenate([zero.astype(a.dtype), a[:, part:]], axis=0)
        return jnp.concatenate([left, right], axis=1)

    exact = strict.astype(BF16)
    power = dot(exact, diagonal(exact))
    result = jnp.where(row == col, 1.0, 0.0) - strict
    repeats = (part - 1).bit_length() - 1
    for repeat in range(repeats):
        pause(repeat)
        multiply = dot_split if repeat < 2 else dot_short
        if repeat == repeats - 1:
            result = result + multiply(result, diagonal(power))
        else:
            both = multiply(jnp.concatenate([result, power], axis=0), diagonal(power))
            result, power = result + both[:part], both[part:]
    upper, lower = result[:, :part], result[:, part:]
    high, low = halves(upper)
    below = full[part:, :part].astype(BF16)
    corner = -dot_split(lower, dot(below, high) + dot(below, low))
    return jnp.concatenate(
        [jnp.concatenate([upper, zero], axis=1), jnp.concatenate([corner, lower], axis=1)], axis=0
    )


def onehot(a, b):
    return (a == b).astype(F32)


def body(
    process_rows, process_cols,
    matrix_hbm, one_hbm, two_hbm, piv_one_hbm, piv_two_hbm, out,
    piv_one, piv_two, matrix, picks, panels, chosen_panel, sent_sel, sel_in,
    rows_part, pair_rows, group_rows, lead, cross, solved, leaving, inverse,
    l_sem, g_send, z_recv, f_recv, x_recv, d_send, d_recv, h_recv, s_send, s_recv,
    p_send, p_recv, q_send, q_recv, i_send, i_recv,
):
    width = piv_one.shape[1]
    rows_dev, cols = matrix.shape
    shard = one_hbm.shape[0]
    half = width // 2
    blocks = rows_dev // width
    size_z = process_cols // 2
    groups = process_rows // 2
    my_row = lax.axis_index("prow")
    my_col = lax.axis_index("pcol")
    my_z, my_x = my_col // 2, my_col % 2
    x_peer = my_z * 2 + (1 - my_x)
    group, core = my_row // 2, my_row % 2
    pair = group * 2 + (1 - core)
    mesh_ids = pl.DeviceIdType.MESH
    panel_hbm = (one_hbm, two_hbm)
    span = [pl.ds(block * width, width) for block in range(blocks)]
    whole, rest = pl.ds(0, rows_dev), pl.ds(width, rows_dev - width)
    top, lower = group == 0, group > 0
    is_zero, is_one, not_one = my_row == 0, my_row == 1, my_row != 1
    lower_zero, lower_one = lower & (core == 0), lower & (core == 1)

    def row_peer(step):
        return lax.rem(my_row + step, process_rows)

    cols_at = [lax.rem(my_col + step, process_cols) for step in range(process_cols)]
    zs_at = [lax.rem(my_z + step, size_z) * 2 + my_x for step in range(size_z)]
    across_at = [lax.rem(my_z + step, size_z) * 2 + (1 - my_x) for step in range(size_z)]
    groups_at = [lax.rem(group + step, groups) * 2 + core for step in range(groups)]
    odd = my_z % 2
    beside = (my_z + 1 - 2 * odd) * 2 + my_x
    at_end = (my_z == 0) | (my_z == size_z - 1)
    by_start, by_end = my_z == 1, my_z == size_z - 2
    near_end = by_start | by_end
    inside = jnp.logical_not(at_end)
    far_start, far_end = my_x, (size_z - 1) * 2 + my_x

    barrier = pltpu.get_barrier_semaphore()
    for step in range(1, process_rows):
        pl.semaphore_signal(barrier, 1, device_id={"prow": row_peer(step)}, device_id_type=mesh_ids)
    for step in range(1, process_cols):
        pl.semaphore_signal(barrier, 1, device_id={"pcol": cols_at[step]}, device_id_type=mesh_ids)

    loads = [
        pltpu.make_async_copy(piv_one_hbm, piv_one, l_sem.at[0]),
        pltpu.make_async_copy(piv_two_hbm, piv_two, l_sem.at[1]),
        pltpu.make_async_copy(one_hbm, panels.at[0, my_col], l_sem.at[2]),
        pltpu.make_async_copy(matrix_hbm, matrix, l_sem.at[3]),
        pltpu.make_async_copy(two_hbm, panels.at[1, my_col], l_sem.at[4]),
    ]
    for load in loads:
        load.start()

    def remote(src, dst, send, recv, device):
        return pltpu.make_async_remote_copy(
            src_ref=src, dst_ref=dst, send_sem=send, recv_sem=recv,
            device_id=device, device_id_type=mesh_ids,
        )

    def arrived(ref, recv):
        remote(ref, ref, g_send, recv, {"pcol": x_peer}).wait_recv()

    def departed(ref, send):
        remote(ref, ref, send, x_recv.at[0], {"pcol": x_peer}).wait_send()

    def place(panel, block, col):
        return panels.at[panel, col, :, span[block]]

    def several(panel, block, count):
        return panels.at[panel, pl.ds(0, count), :, span[block]]

    def along(panel, block, source, col, target):
        remote(
            source, place(panel, block, col), g_send, z_recv.at[panel, block], {"pcol": target}
        ).start()

    def send_z(panel, block):
        for step in reversed(range(1, size_z)):
            across_ends = at_end & ((zs_at[step] // 2 == 0) | (zs_at[step] // 2 == size_z - 1))

            @pl.when(jnp.logical_not(across_ends))
            def _(step=step):
                along(panel, block, panel_hbm[panel].at[:, span[block]], my_col, zs_at[step])

    def send_x(panel, part):
        remote(
            panel_hbm[panel].at[:, part], panels.at[panel, my_col, :, part], g_send, x_recv.at[panel], {"pcol": x_peer}
        ).start()

    def forward(panel, block):
        arrived(several(panel, block, size_z - 1), z_recv.at[panel, block])

        @pl.when(by_end)
        def _():
            along(panel, block, place(panel, block, far_start), far_start, far_end)

        @pl.when(by_start)
        def _():
            along(panel, block, place(panel, block, far_end), far_end, far_start)

        for step in range(1, size_z - panel):
            col = lax.rem(my_z + step + panel * (1 - odd), size_z) * 2 + my_x
            slot = place(panel, block, col)
            remote(slot, slot, g_send, f_recv.at[panel, block], {"pcol": x_peer}).start()

    def forward_if(condition, panel, some):
        @pl.when(condition)
        def _():
            for block in some:
                forward(panel, block)

    def take(panel, block):
        arrived(several(panel, block, size_z - 1 - panel), f_recv.at[panel, block])

    def take_x(panel, part):
        arrived(panels.at[panel, x_peer, :, part], x_recv.at[panel])

    def pass_beside(part):
        take_x(1, part)
        slot = panels.at[1, x_peer, :, part]
        remote(slot, slot, g_send, x_recv.at[2], {"pcol": beside}).start()

    def take_beside(part):
        arrived(panels.at[1, x_peer, :, part], x_recv.at[2])

    def all_departed(part):
        @pl.when(at_end)
        def _():
            departed(panels.at[:, pl.ds(0, process_cols - 2), :, part], g_send)

        @pl.when(near_end)
        def _():
            departed(panels.at[:, :, :, part], g_send)

        @pl.when(inside & jnp.logical_not(near_end))
        def _():
            departed(panels.at[:, pl.ds(0, process_cols - 1), :, part], g_send)

    def direct(index, source, target):
        for step in range(1, process_cols):
            remote(source, target, d_send.at[index], d_recv.at[index], {"pcol": cols_at[step]}).start()

    def spread(index, source, target):
        for step in range(size_z):
            recv = h_recv.at[index] if step else d_recv.at[index]
            remote(source, target, d_send.at[index], recv, {"pcol": zs_at[step] if step else x_peer}).start()

    def spread_on(index):
        arrived(several(index, 0, size_z - 1), h_recv.at[index])
        for step in range(1, size_z):
            slot = place(index, 0, zs_at[step])
            remote(slot, slot, d_send.at[index], d_recv.at[index], {"pcol": x_peer}).start()

    def take_spread(index):
        arrived(several(index, 0, size_z), d_recv.at[index])

    def others():
        return panels.at[0, pl.ds(0, process_cols - 1), :, span[0]]

    def take_direct(index):
        arrived(others(), d_recv.at[index])

    def block_of(panel, block):
        return panels[panel, :, :, span[block]].reshape(width, width)

    def item_copy(item, peer, source=None):
        target = (lead.at[0], lead.at[1], cross, solved.at[0], solved.at[1], leaving)[item]
        return remote(
            target if source is None else source, target, i_send.at[item], i_recv.at[item], {"prow": peer}
        )

    def item_down(item, source=None):
        for step in range(1, groups):
            item_copy(item, groups_at[step], source).start()

    def item_across(item, source=None):
        item_copy(item, pair, source).start()

    def item_wait(item):
        item_copy(item, pair).wait_recv()

    def item_relay(item):
        item_wait(item)
        item_across(item)

    def item_sent(item, copies):
        departed(group_rows.at[pl.ds(0, copies)], i_send.at[item])

    pl.semaphore_wait(barrier, process_rows - 1 + process_cols - 1)

    @pl.when(is_zero)
    def _():
        direct(0, one_hbm.at[:, span[0]], place(0, 0, my_col))
        item_across(LEAD_ONE, matrix_hbm.at[span[0], :])
        item_down(LEAD_ONE, matrix_hbm.at[span[0], :])

    @pl.when(is_one)
    def _():
        spread(1, two_hbm.at[:, span[0]], place(1, 0, my_col))
        spread(0, one_hbm.at[:, span[0]], place(0, 0, my_col))
        send_x(0, rest)

    @pl.when(is_zero)
    def _():
        send_x(0, rest)
        for block in range(1, blocks):
            send_z(0, block)

    @pl.when(lower)
    def _():
        for panel in range(2):
            send_x(panel, whole)
        for block in range(blocks):
            send_z(0, block)

    for load in loads[:3]:
        load.wait()
    local = lax.broadcasted_iota(jnp.int32, (width, width), 0)
    for block in range(blocks):
        hit = onehot(local, piv_two[...] - (block * process_rows + my_row) * width)
        picks[1, span[block], :] = hit.astype(BF16)
    sent_sel[...] = dot(panels[0, my_col], picks[1]).astype(BF16)

    def sel_copy():
        return remote(sent_sel, sel_in.at[my_row], s_send, s_recv, {"prow": 1})

    @pl.when(not_one)
    def _():
        sel_copy().start()

    for block in range(blocks):
        hit = onehot(local, piv_one[...] - (block * process_rows + my_row) * width)
        picks[0, span[block], :] = hit.astype(BF16)
    loads[3].wait()
    for which in range(2):
        rows_part[which] = dot_t(picks[which], matrix[...]).astype(BF16).reshape(2, half, cols)

    def top_copy():
        return remote(rows_part.at[1 - core], pair_rows, p_send, p_recv, {"prow": pair})

    def half_copy():
        return remote(rows_part.at[:, 1 - core], pair_rows, p_send, p_recv, {"prow": pair})

    def rows_copy(which):
        return remote(
            rows_part.at[which, core], group_rows.at[group, core], q_send, q_recv, {"prow": which}
        )

    def swap(which, rows):
        pick = picks[which]
        kept = 1.0 - jnp.sum(pick.astype(F32), axis=1, keepdims=True)
        matrix[...] = (matrix[...].astype(F32) * kept + dot(pick, rows)).astype(BF16)

    def update(panel, block, to):
        to[span[block], :] = (
            matrix[span[block], :].astype(F32) - dot_t(block_of(panel, block), solved[panel])
        ).astype(BF16)

    def chosen():
        total = rows_part[core].astype(F32) + pair_rows[...].astype(F32)
        arrived(group_rows.at[pl.ds(0, groups - 1)], q_recv)
        for source in range(1, groups):
            total = total + group_rows[source].astype(F32)
        return total.astype(BF16).reshape(width, cols)

    def solve(incoming):
        return (dot(inverse[0], incoming) + dot(inverse[1], incoming)).astype(BF16)

    @pl.when(top)
    def _():
        top_copy().start()

    @pl.when(is_zero)
    def _():
        send_x(1, rest)
        for block in range(1, blocks):
            send_z(1, block)
        lead[0] = matrix[span[0], :]
        swap(0, lead[0])

    @pl.when(is_one)
    def _():
        selected = sent_sel[...].astype(F32)
        arrived(sel_in.at[pl.ds(0, process_rows - 1)], s_recv)
        for step in range(1, process_rows):
            selected = selected + sel_in[row_peer(step)].astype(F32)
        chosen_panel[my_col] = selected.astype(BF16)
        direct(2, chosen_panel.at[my_col], chosen_panel.at[my_col])
        for block in range(1, blocks):
            send_z(0, block)
        send_x(1, rest)
        for block in range(1, blocks):
            send_z(1, block)
        spread_on(1)
        item_wait(LEAD_ONE)
        pick = picks[0, span[0], :]
        kept = 1.0 - jnp.sum(pick.astype(F32), axis=1, keepdims=True)
        lead[1] = (matrix[span[0], :].astype(F32) * kept + dot(pick, lead[0])).astype(BF16)
        item_down(LEAD_TWO)
        spread_on(0)
        swap(0, lead[0])

    @pl.when(top)
    def _():
        loads[4].wait()

    @pl.when(is_zero)
    def _():
        take_direct(0)

        def pause(step):
            if step == 4:
                forward_if(inside, 0, (1,))

        result = unit_inverse(block_of(0, 0), pause)
        inverse[0], inverse[1] = halves(result)
        top_copy().wait_recv()
        solved[0] = solve(chosen())
        item_across(SOLVED_ONE)
        item_down(SOLVED_ONE)
        forward_if(at_end, 0, (1,))
        for block in range(2, blocks):
            forward(0, block)

    @pl.when(is_one)
    def _():
        take_spread(1)

        def pause(step):
            pass

        result = unit_inverse(block_of(1, 0), pause)
        inverse[0], inverse[1] = halves(result)
        first_across = jnp.broadcast_to(piv_one[...], (width, width))
        second_down = jnp.broadcast_to(piv_two[...].astype(F32), (width, width)).T.astype(jnp.int32)
        take_spread(0)
        cross[...] = panels[0, :, :, span[0]]
        item_down(CROSS)
        forward_if(inside, 0, range(1, blocks))
        match = onehot(second_down, first_across)
        kept = 1.0 - jnp.sum(match, axis=1, keepdims=True)
        top_copy().wait_recv()
        swapped = chosen().astype(F32) * kept + dot(match.astype(BF16), lead[0])
        take_direct(2)
        item_wait(SOLVED_ONE)
        incoming = (swapped - dot_t(chosen_panel[...].reshape(width, width), solved[0])).astype(BF16)
        solved[1] = solve(incoming)
        item_down(SOLVED_TWO)
        item_across(SOLVED_TWO)
        leaving[...] = (lead[1].astype(F32) - dot_t(block_of(0, 0), solved[0])).astype(BF16)
        item_across(LEAVING_TWO)
        forward_if(at_end, 0, range(1, blocks))

    @pl.when(top)
    def _():
        pass_beside(rest)
        for block in range(1, blocks):
            forward(1, block)
        take_x(0, rest)
        for block in range(1, blocks):
            take(0, block)
            update(0, block, matrix)

    @pl.when(is_zero)
    def _():
        item_wait(LEAVING_TWO)
        swap(1, leaving[...])
        item_wait(SOLVED_TWO)
        out[span[0], :] = solved[0]

    @pl.when(is_one)
    def _():
        swap(1, leaving[...])
        out[span[0], :] = solved[1]

    @pl.when(top)
    def _():
        take_beside(rest)
        for block in range(1, blocks):
            take(1, block)
            update(1, block, out)

    @pl.when(lower)
    def _():
        half_copy().start()
        for block in range(blocks):
            send_z(1, block)
        half_copy().wait_recv()
        for which in range(2):
            rows_part[which, core] = (
                rows_part[which, core].astype(F32) + pair_rows[which].astype(F32)
            ).astype(BF16)
            rows_copy(which).start()
        loads[4].wait()
        forward(0, 0)

    @pl.when(lower_zero)
    def _():
        item_relay(LEAD_ONE)

    @pl.when(lower_one)
    def _():
        item_wait(LEAD_ONE)

    @pl.when(lower)
    def _():
        swap(0, lead[0])
        forward(0, 1)
        pass_beside(whole)
        for block in range(2, blocks):
            forward(0, block)

    @pl.when(lower_one)
    def _():
        item_relay(LEAD_TWO)

    @pl.when(lower)
    def _():
        forward(1, 0)
        forward_if(inside, 1, range(1, blocks))
        forward_if(at_end, 1, (1,))

    @pl.when(lower_one)
    def _():
        item_relay(CROSS)

    @pl.when(lower_zero)
    def _():
        item_relay(SOLVED_ONE)

    @pl.when(lower)
    def _():
        forward_if(at_end, 1, range(2, blocks))

    @pl.when(lower_zero)
    def _():
        item_wait(LEAD_TWO)
        item_wait(CROSS)

    @pl.when(lower_one)
    def _():
        item_relay(SOLVED_TWO)
        item_wait(SOLVED_ONE)

    @pl.when(lower)
    def _():
        take_x(0, whole)
        for block in range(blocks):
            take(0, block)
            update(0, block, matrix)
        leaving[...] = (lead[1].astype(F32) - dot_t(cross[...].reshape(width, width), solved[0])).astype(BF16)
        swap(1, leaving[...])

    @pl.when(lower_zero)
    def _():
        item_wait(SOLVED_TWO)

    @pl.when(lower)
    def _():
        take_beside(whole)
        for block in range(blocks):
            take(1, block)
            update(1, block, out)
        all_departed(whole)
        half_copy().wait_send()
        departed(rows_part.at[:, core], q_send)

    @pl.when(lower_zero)
    def _():
        item_sent(LEAD_ONE, 1)
        item_sent(SOLVED_ONE, 1)

    @pl.when(lower_one)
    def _():
        item_sent(LEAD_TWO, 1)
        item_sent(CROSS, 1)
        item_sent(SOLVED_TWO, 1)

    @pl.when(top)
    def _():
        all_departed(rest)
        top_copy().wait_send()
        departed(others(), d_send.at[0])

    @pl.when(is_zero)
    def _():
        item_sent(LEAD_ONE, groups)
        item_sent(SOLVED_ONE, groups)

    @pl.when(is_one)
    def _():
        departed(others(), d_send.at[1])
        departed(others(), d_send.at[2])
        item_sent(LEAD_TWO, groups - 1)
        item_sent(CROSS, groups - 1)
        item_sent(SOLVED_TWO, groups)
        item_sent(LEAVING_TWO, 1)

    @pl.when(not_one)
    def _():
        sel_copy().wait_send()


def on_device(matrix, panel_one, panel_two, pivots_one, pivots_two):
    process_rows = lax.axis_size("prow")
    process_cols = lax.axis_size("pcol")
    shard, rows_dev = panel_one.shape
    width = pivots_one.shape[0]
    cols = matrix.shape[1]
    vmem = pl.BlockSpec(memory_space=pltpu.VMEM)
    hbm = pl.BlockSpec(memory_space=pltpu.HBM)
    dma = pltpu.SemaphoreType.DMA
    assert rows_dev > width and rows_dev % width == 0 and shard * process_cols == width
    assert process_cols % 4 == 0 and process_cols >= 8 and process_rows % 2 == 0
    groups = process_rows // 2
    blocks = rows_dev // width
    operands = (matrix, panel_one, panel_two, pivots_one.reshape(1, width), pivots_two.reshape(1, width))
    return pl.pallas_call(
        functools.partial(body, process_rows, process_cols),
        out_shape=jax.ShapeDtypeStruct(matrix.shape, BF16),
        in_specs=[hbm] * 5,
        out_specs=vmem,
        scratch_shapes=[
            pltpu.VMEM((1, width), jnp.int32),
            pltpu.VMEM((1, width), jnp.int32),
            pltpu.VMEM((rows_dev, cols), BF16),
            pltpu.VMEM((2, rows_dev, width), BF16),
            pltpu.VMEM((2, process_cols, shard, rows_dev), BF16),
            pltpu.VMEM((process_cols, shard, width), BF16),
            pltpu.VMEM((shard, width), BF16),
            pltpu.VMEM((process_rows, shard, width), BF16),
            pltpu.VMEM((2, 2, width // 2, cols), BF16),
            pltpu.VMEM((2, width // 2, cols), BF16),
            pltpu.VMEM((groups, 2, width // 2, cols), BF16),
            pltpu.VMEM((2, width, cols), BF16),
            pltpu.VMEM((process_cols, shard, width), BF16),
            pltpu.VMEM((2, width, cols), BF16),
            pltpu.VMEM((width, cols), BF16),
            pltpu.VMEM((2, width, width), BF16),
            dma((5,)),
            dma, dma((2, blocks)), dma((2, blocks)), dma((3,)),
            dma((3,)), dma((3,)), dma((2,)),
            dma, dma,
            dma, dma,
            dma, dma,
            dma((6,)), dma((6,)),
        ],
        compiler_params=pltpu.CompilerParams(
            collective_id=0, has_side_effects=True, vmem_limit_bytes=32 * 1024 * 1024
        ),
    )(*[pltpu.with_memory_space_constraint(operand, pltpu.HBM) for operand in operands])


def solution(mesh):
    placed = (P("prow", "pcol"), P("pcol", "prow"), P("pcol", "prow"), P(), P())
    return jax.shard_map(
        on_device, mesh=mesh, in_specs=placed, out_specs=P("prow", "pcol"), check_vma=False
    )
```

```python
import functools

import jax
import jax.numpy as jnp
from jax import lax
from jax.experimental import pallas as pl
from jax.experimental.pallas import tpu as pltpu
from jax.sharding import PartitionSpec as P

F32 = jnp.float32
BF16 = jnp.bfloat16
ROW_ROW = (((0,), (0,)), ((), ()))
LEAD_ONE, LEAD_TWO, CROSS, SOLVED_ONE, SOLVED_TWO, LEAVING_TWO = range(6)


def dot(a, b):
    return jnp.dot(a, b, preferred_element_type=F32)


def dot_t(a, b):
    return lax.dot_general(a, b, ROW_ROW, preferred_element_type=F32)


def halves(a):
    high = a.astype(BF16)
    return high, (a - high.astype(F32)).astype(BF16)


def dot_split(a, b):
    a_high, a_low = halves(a)
    b_high, b_low = halves(b)
    return dot(a_high, b_high) + (dot(a_high, b_low) + dot(a_low, b_high))


def dot_short(a, b):
    return dot(a.astype(BF16), b.astype(BF16))


def unit_inverse(panel, pause):
    extent = panel.shape[0]
    part = extent // 2
    full = panel.astype(F32).T
    row = lax.broadcasted_iota(jnp.int32, (part, extent), 0)
    col = lax.broadcasted_iota(jnp.int32, (part, extent), 1) % part
    strict = jnp.where(row > col, jnp.concatenate([full[:part, :part], full[part:, part:]], axis=1), 0.0)
    zero = jnp.zeros((part, part), F32)

    def diagonal(a):
        left = jnp.concatenate([a[:, :part], zero.astype(a.dtype)], axis=0)
        right = jnp.concatenate([zero.astype(a.dtype), a[:, part:]], axis=0)
        return jnp.concatenate([left, right], axis=1)

    exact = strict.astype(BF16)
    power = dot(exact, diagonal(exact))
    result = jnp.where(row == col, 1.0, 0.0) - strict
    repeats = (part - 1).bit_length() - 1
    for repeat in range(repeats):
        pause(repeat)
        multiply = dot_split if repeat < 2 else dot_short
        if repeat == repeats - 1:
            result = result + multiply(result, diagonal(power))
        else:
            both = multiply(jnp.concatenate([result, power], axis=0), diagonal(power))
            result, power = result + both[:part], both[part:]
    upper, lower = result[:, :part], result[:, part:]
    high, low = halves(upper)
    below = full[part:, :part].astype(BF16)
    corner = -dot_split(lower, dot(below, high) + dot(below, low))
    return jnp.concatenate(
        [jnp.concatenate([upper, zero], axis=1), jnp.concatenate([corner, lower], axis=1)], axis=0
    )


def onehot(a, b):
    return (a == b).astype(F32)


def body(
    process_rows, process_cols,
    matrix_hbm, one_hbm, two_hbm, piv_one_hbm, piv_two_hbm, out,
    piv_one, piv_two, matrix, picks, panels, chosen_panel, sent_sel, sel_in,
    rows_part, pair_rows, group_rows, lead, cross, solved, leaving, inverse,
    l_sem, g_send, z_recv, f_recv, x_recv, d_send, d_recv, h_recv, s_send, s_recv,
    p_send, p_recv, q_send, q_recv, i_send, i_recv,
):
    width = piv_one.shape[1]
    rows_dev, cols = matrix.shape
    shard = one_hbm.shape[0]
    half = width // 2
    blocks = rows_dev // width
    size_z = process_cols // 2
    groups = process_rows // 2
    my_row = lax.axis_index("prow")
    my_col = lax.axis_index("pcol")
    my_z, my_x = my_col // 2, my_col % 2
    x_peer = my_z * 2 + (1 - my_x)
    group, core = my_row // 2, my_row % 2
    pair = group * 2 + (1 - core)
    mesh_ids = pl.DeviceIdType.MESH
    panel_hbm = (one_hbm, two_hbm)
    span = [pl.ds(block * width, width) for block in range(blocks)]
    whole, rest = pl.ds(0, rows_dev), pl.ds(width, rows_dev - width)
    top, lower = group == 0, group > 0
    is_zero, is_one, not_one = my_row == 0, my_row == 1, my_row != 1
    lower_zero, lower_one = lower & (core == 0), lower & (core == 1)

    def row_peer(step):
        return lax.rem(my_row + step, process_rows)

    cols_at = [lax.rem(my_col + step, process_cols) for step in range(process_cols)]
    zs_at = [lax.rem(my_z + step, size_z) * 2 + my_x for step in range(size_z)]
    across_at = [lax.rem(my_z + step, size_z) * 2 + (1 - my_x) for step in range(size_z)]
    groups_at = [lax.rem(group + step, groups) * 2 + core for step in range(groups)]
    ends_at = [(col // 2 == 0) | (col // 2 == size_z - 1) for col in zs_at]
    odd = my_z % 2
    beside = (my_z + 1 - 2 * odd) * 2 + my_x
    at_end = (my_z == 0) | (my_z == size_z - 1)
    by_start, by_end = my_z == 1, my_z == size_z - 2
    near_end = by_start | by_end
    inside = jnp.logical_not(at_end)
    far_start, far_end = my_x, (size_z - 1) * 2 + my_x

    barrier = pltpu.get_barrier_semaphore()
    for step in range(1, process_rows):
        pl.semaphore_signal(barrier, 1, device_id={"prow": row_peer(step)}, device_id_type=mesh_ids)
    for step in range(1, process_cols):
        pl.semaphore_signal(barrier, 1, device_id={"pcol": cols_at[step]}, device_id_type=mesh_ids)

    loads = [
        pltpu.make_async_copy(piv_one_hbm, piv_one, l_sem.at[0]),
        pltpu.make_async_copy(piv_two_hbm, piv_two, l_sem.at[1]),
        pltpu.make_async_copy(one_hbm, panels.at[0, my_col], l_sem.at[2]),
        pltpu.make_async_copy(matrix_hbm, matrix, l_sem.at[3]),
        pltpu.make_async_copy(two_hbm, panels.at[1, my_col], l_sem.at[4]),
    ]
    for load in loads:
        load.start()

    def remote(src, dst, send, recv, device):
        return pltpu.make_async_remote_copy(
            src_ref=src, dst_ref=dst, send_sem=send, recv_sem=recv,
            device_id=device, device_id_type=mesh_ids,
        )

    def arrived(ref, recv):
        remote(ref, ref, g_send.at[0], recv, {"pcol": x_peer}).wait_recv()

    def departed(ref, send):
        remote(ref, ref, send, x_recv.at[0], {"pcol": x_peer}).wait_send()

    def place(panel, block, col):
        return panels.at[panel, col, :, span[block]]

    def several(panel, block, count):
        return panels.at[panel, pl.ds(0, count), :, span[block]]

    def along(panel, block, source, col, target):
        remote(
            source, place(panel, block, col), g_send.at[panel], z_recv.at[panel, block], {"pcol": target}
        ).start()

    def relayed(panel):
        return lower if panel else my_row >= 0

    def send_z(panel, block):
        for step in reversed(range(1, size_z)):
            def send(step=step):
                along(panel, block, panel_hbm[panel].at[:, span[block]], my_col, zs_at[step])

            pl.when(jnp.logical_not(relayed(panel) & at_end & ends_at[step]))(send)

    def send_x(panel, part):
        remote(
            panel_hbm[panel].at[:, part], panels.at[panel, my_col, :, part], g_send.at[panel], x_recv.at[panel], {"pcol": x_peer}
        ).start()

    def forward(panel, block):
        arrived(several(panel, block, size_z - 1), z_recv.at[panel, block])

        @pl.when(by_end & relayed(panel))
        def _():
            along(panel, block, place(panel, block, far_start), far_start, far_end)

        @pl.when(by_start & relayed(panel))
        def _():
            along(panel, block, place(panel, block, far_end), far_end, far_start)

        for step in range(1, size_z - panel):
            col = lax.rem(my_z + step + panel * (1 - odd), size_z) * 2 + my_x
            slot = place(panel, block, col)
            remote(slot, slot, g_send.at[panel], f_recv.at[panel, block], {"pcol": x_peer}).start()

    def forward_if(condition, panel, some):
        @pl.when(condition)
        def _():
            for block in some:
                forward(panel, block)

    def take(panel, block):
        arrived(several(panel, block, size_z - 1 - panel), f_recv.at[panel, block])

    def take_x(panel, part):
        arrived(panels.at[panel, x_peer, :, part], x_recv.at[panel])

    def pass_beside(part):
        take_x(1, part)
        slot = panels.at[1, x_peer, :, part]
        remote(slot, slot, g_send.at[1], x_recv.at[2], {"pcol": beside}).start()

    def take_beside(part):
        arrived(panels.at[1, x_peer, :, part], x_recv.at[2])

    def all_departed(part):
        for panel in range(2):
            fewer, more = relayed(panel) & at_end, relayed(panel) & near_end

            @pl.when(fewer)
            def _(panel=panel):
                departed(panels.at[panel, pl.ds(0, process_cols - 2), :, part], g_send.at[panel])

            @pl.when(more)
            def _(panel=panel):
                departed(panels.at[panel, :, :, part], g_send.at[panel])

            @pl.when(jnp.logical_not(fewer | more))
            def _(panel=panel):
                departed(panels.at[panel, pl.ds(0, process_cols - 1), :, part], g_send.at[panel])

    def direct(index, source, target):
        for step in range(1, process_cols):
            remote(source, target, d_send.at[index], d_recv.at[index], {"pcol": cols_at[step]}).start()

    def spread(index, source, target):
        for step in range(size_z):
            recv = h_recv.at[index] if step else d_recv.at[index]
            remote(source, target, d_send.at[index], recv, {"pcol": zs_at[step] if step else x_peer}).start()

    def spread_on(index):
        arrived(several(0, 0, size_z - 1), h_recv.at[index])
        for step in range(1, size_z):
            slot = chosen_panel.at[zs_at[step]] if index == 2 else place(index, 0, zs_at[step])
            remote(slot, slot, d_send.at[index], d_recv.at[index], {"pcol": x_peer}).start()

    def take_spread(index):
        arrived(several(0, 0, size_z), d_recv.at[index])

    def others():
        return panels.at[0, pl.ds(0, process_cols - 1), :, span[0]]

    def take_direct(index):
        arrived(others(), d_recv.at[index])

    def block_of(panel, block):
        return panels[panel, :, :, span[block]].reshape(width, width)

    def item_copy(item, peer, source=None):
        target = (lead.at[0], lead.at[1], cross, solved.at[0], solved.at[1], leaving)[item]
        return remote(
            target if source is None else source, target, i_send.at[item], i_recv.at[item], {"prow": peer}
        )

    def item_down(item, source=None):
        for step in range(1, groups):
            item_copy(item, groups_at[step], source).start()

    def item_across(item, source=None):
        item_copy(item, pair, source).start()

    def item_wait(item):
        item_copy(item, pair).wait_recv()

    def item_relay(item):
        item_wait(item)
        item_across(item)

    def item_sent(item, copies):
        departed(group_rows.at[pl.ds(0, copies)], i_send.at[item])

    pl.semaphore_wait(barrier, process_rows - 1 + process_cols - 1)

    @pl.when(is_zero)
    def _():
        direct(0, one_hbm.at[:, span[0]], place(0, 0, my_col))
        item_across(LEAD_ONE, matrix_hbm.at[span[0], :])
        item_down(LEAD_ONE, matrix_hbm.at[span[0], :])

    @pl.when(is_one)
    def _():
        spread(1, two_hbm.at[:, span[0]], place(1, 0, my_col))
        spread(0, one_hbm.at[:, span[0]], place(0, 0, my_col))
        send_x(0, rest)

    @pl.when(is_zero)
    def _():
        send_x(0, rest)
        for block in range(1, blocks):
            send_z(0, block)

    @pl.when(lower)
    def _():
        for panel in range(2):
            send_x(panel, whole)
        for block in range(blocks):
            send_z(0, block)

    for load in loads[:3]:
        load.wait()
    local = lax.broadcasted_iota(jnp.int32, (width, width), 0)
    for block in range(blocks):
        hit = onehot(local, piv_two[...] - (block * process_rows + my_row) * width)
        picks[1, span[block], :] = hit.astype(BF16)
    sent_sel[...] = dot(panels[0, my_col], picks[1]).astype(BF16)

    def sel_copy():
        return remote(sent_sel, sel_in.at[my_row], s_send, s_recv, {"prow": 1})

    @pl.when(not_one)
    def _():
        sel_copy().start()

    for block in range(blocks):
        hit = onehot(local, piv_one[...] - (block * process_rows + my_row) * width)
        picks[0, span[block], :] = hit.astype(BF16)
    loads[3].wait()
    for which in range(2):
        rows_part[which] = dot_t(picks[which], matrix[...]).astype(BF16).reshape(2, half, cols)

    def top_copy():
        return remote(rows_part.at[1 - core], pair_rows, p_send, p_recv, {"prow": pair})

    def half_copy():
        return remote(rows_part.at[:, 1 - core], pair_rows, p_send, p_recv, {"prow": pair})

    def rows_copy(which):
        return remote(
            rows_part.at[which, core], group_rows.at[group, core], q_send, q_recv, {"prow": which}
        )

    def swap(which, rows):
        pick = picks[which]
        kept = 1.0 - jnp.sum(pick.astype(F32), axis=1, keepdims=True)
        matrix[...] = (matrix[...].astype(F32) * kept + dot(pick, rows)).astype(BF16)

    def update(panel, block, to):
        to[span[block], :] = (
            matrix[span[block], :].astype(F32) - dot_t(block_of(panel, block), solved[panel])
        ).astype(BF16)

    def chosen():
        total = rows_part[core].astype(F32) + pair_rows[...].astype(F32)
        arrived(group_rows.at[pl.ds(0, groups - 1)], q_recv)
        for source in range(1, groups):
            total = total + group_rows[source].astype(F32)
        return total.astype(BF16).reshape(width, cols)

    def solve(incoming):
        return (dot(inverse[0], incoming) + dot(inverse[1], incoming)).astype(BF16)

    @pl.when(top)
    def _():
        top_copy().start()

    @pl.when(is_zero)
    def _():
        send_x(1, rest)
        for block in range(1, blocks):
            send_z(1, block)
        lead[0] = matrix[span[0], :]
        swap(0, lead[0])

    @pl.when(is_one)
    def _():
        selected = sent_sel[...].astype(F32)
        arrived(sel_in.at[pl.ds(0, process_rows - 1)], s_recv)
        for step in range(1, process_rows):
            selected = selected + sel_in[row_peer(step)].astype(F32)
        chosen_panel[my_col] = selected.astype(BF16)
        spread(2, chosen_panel.at[my_col], chosen_panel.at[my_col])
        for block in range(1, blocks):
            send_z(0, block)
        send_x(1, rest)
        for block in range(1, blocks):
            send_z(1, block)
        spread_on(1)
        item_wait(LEAD_ONE)
        pick = picks[0, span[0], :]
        kept = 1.0 - jnp.sum(pick.astype(F32), axis=1, keepdims=True)
        lead[1] = (matrix[span[0], :].astype(F32) * kept + dot(pick, lead[0])).astype(BF16)
        item_down(LEAD_TWO)
        spread_on(0)
        swap(0, lead[0])

    @pl.when(top)
    def _():
        loads[4].wait()

    @pl.when(is_zero)
    def _():
        take_direct(0)

        def pause(step):
            if step == 4:
                forward_if(inside, 0, (1,))

        result = unit_inverse(block_of(0, 0), pause)
        inverse[0], inverse[1] = halves(result)
        top_copy().wait_recv()
        solved[0] = solve(chosen())
        item_across(SOLVED_ONE)
        item_down(SOLVED_ONE)
        forward_if(at_end, 0, (1,))
        for block in range(2, blocks):
            forward(0, block)

    @pl.when(is_one)
    def _():
        spread_on(2)
        take_spread(1)

        def pause(step):
            pass

        result = unit_inverse(block_of(1, 0), pause)
        inverse[0], inverse[1] = halves(result)
        first_across = jnp.broadcast_to(piv_one[...], (width, width))
        second_down = jnp.broadcast_to(piv_two[...].astype(F32), (width, width)).T.astype(jnp.int32)
        take_spread(0)
        cross[...] = panels[0, :, :, span[0]]
        item_down(CROSS)
        forward_if(inside, 0, range(1, blocks))
        match = onehot(second_down, first_across)
        kept = 1.0 - jnp.sum(match, axis=1, keepdims=True)
        top_copy().wait_recv()
        swapped = chosen().astype(F32) * kept + dot(match.astype(BF16), lead[0])
        take_spread(2)
        item_wait(SOLVED_ONE)
        incoming = (swapped - dot_t(chosen_panel[...].reshape(width, width), solved[0])).astype(BF16)
        solved[1] = solve(incoming)
        item_down(SOLVED_TWO)
        item_across(SOLVED_TWO)
        leaving[...] = (lead[1].astype(F32) - dot_t(block_of(0, 0), solved[0])).astype(BF16)
        item_across(LEAVING_TWO)
        forward_if(at_end, 0, range(1, blocks))

    @pl.when(top)
    def _():
        pass_beside(rest)
        for block in range(1, blocks):
            forward(1, block)
        take_x(0, rest)
        for block in range(1, blocks):
            take(0, block)
            update(0, block, matrix)

    @pl.when(is_zero)
    def _():
        item_wait(LEAVING_TWO)
        swap(1, leaving[...])
        item_wait(SOLVED_TWO)
        out[span[0], :] = solved[0]

    @pl.when(is_one)
    def _():
        swap(1, leaving[...])
        out[span[0], :] = solved[1]

    @pl.when(top)
    def _():
        take_beside(rest)
        for block in range(1, blocks):
            take(1, block)
            update(1, block, out)

    @pl.when(lower)
    def _():
        half_copy().start()
        for block in range(blocks):
            send_z(1, block)
        half_copy().wait_recv()
        for which in range(2):
            rows_part[which, core] = (
                rows_part[which, core].astype(F32) + pair_rows[which].astype(F32)
            ).astype(BF16)
            rows_copy(which).start()
        loads[4].wait()
        forward(0, 0)

    @pl.when(lower_zero)
    def _():
        item_relay(LEAD_ONE)

    @pl.when(lower_one)
    def _():
        item_wait(LEAD_ONE)

    @pl.when(lower)
    def _():
        swap(0, lead[0])
        forward(0, 1)
        pass_beside(whole)
        for block in range(2, blocks):
            forward(0, block)

    @pl.when(lower_one)
    def _():
        item_relay(LEAD_TWO)

    @pl.when(lower)
    def _():
        forward(1, 0)
        forward_if(inside, 1, range(1, blocks))
        forward_if(at_end, 1, (1,))

    @pl.when(lower_one)
    def _():
        item_relay(CROSS)

    @pl.when(lower_zero)
    def _():
        item_relay(SOLVED_ONE)

    @pl.when(lower)
    def _():
        forward_if(at_end, 1, range(2, blocks))

    @pl.when(lower_zero)
    def _():
        item_wait(LEAD_TWO)
        item_wait(CROSS)

    @pl.when(lower_one)
    def _():
        item_relay(SOLVED_TWO)
        item_wait(SOLVED_ONE)

    @pl.when(lower)
    def _():
        take_x(0, whole)
        for block in range(blocks):
            take(0, block)
            update(0, block, matrix)
        leaving[...] = (lead[1].astype(F32) - dot_t(cross[...].reshape(width, width), solved[0])).astype(BF16)
        swap(1, leaving[...])

    @pl.when(lower_zero)
    def _():
        item_wait(SOLVED_TWO)

    @pl.when(lower)
    def _():
        take_beside(whole)
        for block in range(blocks):
            take(1, block)
            update(1, block, out)
        all_departed(whole)
        half_copy().wait_send()
        departed(rows_part.at[:, core], q_send)

    @pl.when(lower_zero)
    def _():
        item_sent(LEAD_ONE, 1)
        item_sent(SOLVED_ONE, 1)

    @pl.when(lower_one)
    def _():
        item_sent(LEAD_TWO, 1)
        item_sent(CROSS, 1)
        item_sent(SOLVED_TWO, 1)

    @pl.when(top)
    def _():
        all_departed(rest)
        top_copy().wait_send()
        departed(others(), d_send.at[0])

    @pl.when(is_zero)
    def _():
        item_sent(LEAD_ONE, groups)
        item_sent(SOLVED_ONE, groups)

    @pl.when(is_one)
    def _():
        departed(others(), d_send.at[1])
        departed(others(), d_send.at[2])
        item_sent(LEAD_TWO, groups - 1)
        item_sent(CROSS, groups - 1)
        item_sent(SOLVED_TWO, groups)
        item_sent(LEAVING_TWO, 1)

    @pl.when(not_one)
    def _():
        sel_copy().wait_send()


def on_device(matrix, panel_one, panel_two, pivots_one, pivots_two):
    process_rows = lax.axis_size("prow")
    process_cols = lax.axis_size("pcol")
    shard, rows_dev = panel_one.shape
    width = pivots_one.shape[0]
    cols = matrix.shape[1]
    vmem = pl.BlockSpec(memory_space=pltpu.VMEM)
    hbm = pl.BlockSpec(memory_space=pltpu.HBM)
    dma = pltpu.SemaphoreType.DMA
    assert rows_dev > width and rows_dev % width == 0 and shard * process_cols == width
    assert process_cols % 4 == 0 and process_cols >= 8 and process_rows % 2 == 0
    groups = process_rows // 2
    blocks = rows_dev // width
    operands = (matrix, panel_one, panel_two, pivots_one.reshape(1, width), pivots_two.reshape(1, width))
    return pl.pallas_call(
        functools.partial(body, process_rows, process_cols),
        out_shape=jax.ShapeDtypeStruct(matrix.shape, BF16),
        in_specs=[hbm] * 5,
        out_specs=vmem,
        scratch_shapes=[
            pltpu.VMEM((1, width), jnp.int32),
            pltpu.VMEM((1, width), jnp.int32),
            pltpu.VMEM((rows_dev, cols), BF16),
            pltpu.VMEM((2, rows_dev, width), BF16),
            pltpu.VMEM((2, process_cols, shard, rows_dev), BF16),
            pltpu.VMEM((process_cols, shard, width), BF16),
            pltpu.VMEM((shard, width), BF16),
            pltpu.VMEM((process_rows, shard, width), BF16),
            pltpu.VMEM((2, 2, width // 2, cols), BF16),
            pltpu.VMEM((2, width // 2, cols), BF16),
            pltpu.VMEM((groups, 2, width // 2, cols), BF16),
            pltpu.VMEM((2, width, cols), BF16),
            pltpu.VMEM((process_cols, shard, width), BF16),
            pltpu.VMEM((2, width, cols), BF16),
            pltpu.VMEM((width, cols), BF16),
            pltpu.VMEM((2, width, width), BF16),
            dma((5,)),
            dma((2,)), dma((2, blocks)), dma((2, blocks)), dma((3,)),
            dma((3,)), dma((3,)), dma((3,)),
            dma, dma,
            dma, dma,
            dma, dma,
            dma((6,)), dma((6,)),
        ],
        compiler_params=pltpu.CompilerParams(
            collective_id=0, has_side_effects=True, vmem_limit_bytes=32 * 1024 * 1024
        ),
    )(*[pltpu.with_memory_space_constraint(operand, pltpu.HBM) for operand in operands])


def solution(mesh):
    placed = (P("prow", "pcol"), P("pcol", "prow"), P("pcol", "prow"), P(), P())
    return jax.shard_map(
        on_device, mesh=mesh, in_specs=placed, out_specs=P("prow", "pcol"), check_vma=False
    )
```

```python
import functools

import jax
import jax.numpy as jnp
from jax import lax
from jax.experimental import pallas as pl
from jax.experimental.pallas import tpu as pltpu
from jax.sharding import PartitionSpec as P

F32 = jnp.float32
BF16 = jnp.bfloat16
ROW_ROW = (((0,), (0,)), ((), ()))
LEAD_ONE, LEAD_TWO, CROSS, SOLVED_ONE, SOLVED_TWO, LEAVING_TWO = range(6)


def dot(a, b):
    return jnp.dot(a, b, preferred_element_type=F32)


def dot_t(a, b):
    return lax.dot_general(a, b, ROW_ROW, preferred_element_type=F32)


def halves(a):
    high = a.astype(BF16)
    return high, (a - high.astype(F32)).astype(BF16)


def dot_split(a, b):
    a_high, a_low = halves(a)
    b_high, b_low = halves(b)
    return dot(a_high, b_high) + (dot(a_high, b_low) + dot(a_low, b_high))


def dot_short(a, b):
    return dot(a.astype(BF16), b.astype(BF16))


def unit_inverse(panel, pause):
    extent = panel.shape[0]
    part = extent // 2
    full = panel.astype(F32).T
    row = lax.broadcasted_iota(jnp.int32, (part, extent), 0)
    col = lax.broadcasted_iota(jnp.int32, (part, extent), 1) % part
    strict = jnp.where(row > col, jnp.concatenate([full[:part, :part], full[part:, part:]], axis=1), 0.0)
    zero = jnp.zeros((part, part), F32)

    def diagonal(a):
        left = jnp.concatenate([a[:, :part], zero.astype(a.dtype)], axis=0)
        right = jnp.concatenate([zero.astype(a.dtype), a[:, part:]], axis=0)
        return jnp.concatenate([left, right], axis=1)

    exact = strict.astype(BF16)
    power = dot(exact, diagonal(exact))
    result = jnp.where(row == col, 1.0, 0.0) - strict
    repeats = (part - 1).bit_length() - 1
    for repeat in range(repeats):
        pause(repeat)
        multiply = dot_split if repeat < 2 else dot_short
        if repeat == repeats - 1:
            result = result + multiply(result, diagonal(power))
        else:
            both = multiply(jnp.concatenate([result, power], axis=0), diagonal(power))
            result, power = result + both[:part], both[part:]
    upper, lower = result[:, :part], result[:, part:]
    high, low = halves(upper)
    below = full[part:, :part].astype(BF16)
    corner = -dot_split(lower, dot(below, high) + dot(below, low))
    return jnp.concatenate(
        [jnp.concatenate([upper, zero], axis=1), jnp.concatenate([corner, lower], axis=1)], axis=0
    )


def onehot(a, b):
    return (a == b).astype(F32)


def body(
    process_rows, process_cols,
    matrix_hbm, one_hbm, two_hbm, piv_one_hbm, piv_two_hbm, out,
    piv_one, piv_two, matrix, picks, panels, chosen_panel, sent_sel, sel_in,
    rows_part, pair_rows, group_rows, lead, cross, solved, leaving, inverse,
    l_sem, g_send, z_recv, f_recv, x_recv, d_send, d_recv, h_recv, s_send, s_recv,
    p_send, p_recv, q_send, q_recv, i_send, i_recv,
):
    width = piv_one.shape[1]
    rows_dev, cols = matrix.shape
    shard = one_hbm.shape[0]
    half = width // 2
    blocks = rows_dev // width
    size_z = process_cols // 2
    groups = process_rows // 2
    my_row = lax.axis_index("prow")
    my_col = lax.axis_index("pcol")
    my_z, my_x = my_col // 2, my_col % 2
    x_peer = my_z * 2 + (1 - my_x)
    group, core = my_row // 2, my_row % 2
    pair = group * 2 + (1 - core)
    mesh_ids = pl.DeviceIdType.MESH
    panel_hbm = (one_hbm, two_hbm)
    span = [pl.ds(block * width, width) for block in range(blocks)]
    whole, rest = pl.ds(0, rows_dev), pl.ds(width, rows_dev - width)
    top, lower = group == 0, group > 0
    is_zero, is_one, not_one = my_row == 0, my_row == 1, my_row != 1
    lower_zero, lower_one = lower & (core == 0), lower & (core == 1)

    def row_peer(step):
        return lax.rem(my_row + step, process_rows)

    cols_at = [lax.rem(my_col + step, process_cols) for step in range(process_cols)]
    zs_at = [lax.rem(my_z + step, size_z) * 2 + my_x for step in range(size_z)]
    across_at = [lax.rem(my_z + step, size_z) * 2 + (1 - my_x) for step in range(size_z)]
    groups_at = [lax.rem(group + step, groups) * 2 + core for step in range(groups)]
    ends_at = [(col // 2 == 0) | (col // 2 == size_z - 1) for col in zs_at]
    odd = my_z % 2
    beside = (my_z + 1 - 2 * odd) * 2 + my_x
    at_end = (my_z == 0) | (my_z == size_z - 1)
    by_start, by_end = my_z == 1, my_z == size_z - 2
    near_end = by_start | by_end
    inside = jnp.logical_not(at_end)
    far_start, far_end = my_x, (size_z - 1) * 2 + my_x

    barrier = pltpu.get_barrier_semaphore()
    for step in range(1, process_rows):
        pl.semaphore_signal(barrier, 1, device_id={"prow": row_peer(step)}, device_id_type=mesh_ids)
    greeted = process_rows - 1 + jnp.where(is_zero, process_cols - 1, size_z)

    def greet(cols):
        for col in cols:
            pl.semaphore_signal(barrier, 1, device_id={"pcol": col}, device_id_type=mesh_ids)

    @pl.when(is_zero)
    def _():
        greet(cols_at[1:])

    @pl.when(jnp.logical_not(is_zero))
    def _():
        greet([x_peer, *zs_at[1:]])

    loads = [
        pltpu.make_async_copy(piv_one_hbm, piv_one, l_sem.at[0]),
        pltpu.make_async_copy(piv_two_hbm, piv_two, l_sem.at[1]),
        pltpu.make_async_copy(one_hbm, panels.at[0, my_col], l_sem.at[2]),
        pltpu.make_async_copy(matrix_hbm, matrix, l_sem.at[3]),
        pltpu.make_async_copy(two_hbm, panels.at[1, my_col], l_sem.at[4]),
    ]
    for load in loads:
        load.start()

    def remote(src, dst, send, recv, device):
        return pltpu.make_async_remote_copy(
            src_ref=src, dst_ref=dst, send_sem=send, recv_sem=recv,
            device_id=device, device_id_type=mesh_ids,
        )

    def arrived(ref, recv):
        remote(ref, ref, g_send.at[0], recv, {"pcol": x_peer}).wait_recv()

    def departed(ref, send):
        remote(ref, ref, send, x_recv.at[0], {"pcol": x_peer}).wait_send()

    def place(panel, block, col):
        return panels.at[panel, col, :, span[block]]

    def several(panel, block, count):
        return panels.at[panel, pl.ds(0, count), :, span[block]]

    def along(panel, block, source, col, target):
        remote(
            source, place(panel, block, col), g_send.at[panel], z_recv.at[panel, block], {"pcol": target}
        ).start()

    def relayed(panel):
        return lower if panel else my_row >= 0

    def send_z(panel, block):
        for step in reversed(range(1, size_z)):
            def send(step=step):
                along(panel, block, panel_hbm[panel].at[:, span[block]], my_col, zs_at[step])

            pl.when(jnp.logical_not(relayed(panel) & at_end & ends_at[step]))(send)

    def send_x(panel, part):
        remote(
            panel_hbm[panel].at[:, part], panels.at[panel, my_col, :, part], g_send.at[panel], x_recv.at[panel], {"pcol": x_peer}
        ).start()

    def forward(panel, block):
        arrived(several(panel, block, size_z - 1), z_recv.at[panel, block])

        @pl.when(by_end & relayed(panel))
        def _():
            along(panel, block, place(panel, block, far_start), far_start, far_end)

        @pl.when(by_start & relayed(panel))
        def _():
            along(panel, block, place(panel, block, far_end), far_end, far_start)

        for step in range(1, size_z - panel):
            col = lax.rem(my_z + step + panel * (1 - odd), size_z) * 2 + my_x
            slot = place(panel, block, col)
            remote(slot, slot, g_send.at[panel], f_recv.at[panel, block], {"pcol": x_peer}).start()

    def forward_if(condition, panel, some):
        @pl.when(condition)
        def _():
            for block in some:
                forward(panel, block)

    def take(panel, block):
        arrived(several(panel, block, size_z - 1 - panel), f_recv.at[panel, block])

    def take_x(panel, part):
        arrived(panels.at[panel, x_peer, :, part], x_recv.at[panel])

    def pass_beside(part):
        take_x(1, part)
        slot = panels.at[1, x_peer, :, part]
        remote(slot, slot, g_send.at[1], x_recv.at[2], {"pcol": beside}).start()

    def take_beside(part):
        arrived(panels.at[1, x_peer, :, part], x_recv.at[2])

    def all_departed(part):
        for panel in range(2):
            fewer, more = relayed(panel) & at_end, relayed(panel) & near_end

            @pl.when(fewer)
            def _(panel=panel):
                departed(panels.at[panel, pl.ds(0, process_cols - 2), :, part], g_send.at[panel])

            @pl.when(more)
            def _(panel=panel):
                departed(panels.at[panel, :, :, part], g_send.at[panel])

            @pl.when(jnp.logical_not(fewer | more))
            def _(panel=panel):
                departed(panels.at[panel, pl.ds(0, process_cols - 1), :, part], g_send.at[panel])

    def direct(index, source, target):
        for step in range(1, process_cols):
            remote(source, target, d_send.at[index], d_recv.at[index], {"pcol": cols_at[step]}).start()

    def spread(index, source, target):
        for step in range(size_z):
            recv = h_recv.at[index] if step else d_recv.at[index]
            remote(source, target, d_send.at[index], recv, {"pcol": zs_at[step] if step else x_peer}).start()

    def spread_on(index):
        arrived(several(0, 0, size_z - 1), h_recv.at[index])
        for step in range(1, size_z):
            slot = chosen_panel.at[zs_at[step]] if index == 2 else place(index, 0, zs_at[step])
            remote(slot, slot, d_send.at[index], d_recv.at[index], {"pcol": x_peer}).start()

    def take_spread(index):
        arrived(several(0, 0, size_z), d_recv.at[index])

    def others():
        return panels.at[0, pl.ds(0, process_cols - 1), :, span[0]]

    def take_direct(index):
        arrived(others(), d_recv.at[index])

    def block_of(panel, block):
        return panels[panel, :, :, span[block]].reshape(width, width)

    def item_copy(item, peer, source=None):
        target = (lead.at[0], lead.at[1], cross, solved.at[0], solved.at[1], leaving)[item]
        return remote(
            target if source is None else source, target, i_send.at[item], i_recv.at[item], {"prow": peer}
        )

    def item_down(item, source=None):
        for step in range(1, groups):
            item_copy(item, groups_at[step], source).start()

    def item_across(item, source=None):
        item_copy(item, pair, source).start()

    def item_wait(item):
        item_copy(item, pair).wait_recv()

    def item_relay(item):
        item_wait(item)
        item_across(item)

    def item_sent(item, copies):
        departed(group_rows.at[pl.ds(0, copies)], i_send.at[item])

    pl.semaphore_wait(barrier, greeted)

    @pl.when(is_zero)
    def _():
        direct(0, one_hbm.at[:, span[0]], place(0, 0, my_col))
        item_across(LEAD_ONE, matrix_hbm.at[span[0], :])
        item_down(LEAD_ONE, matrix_hbm.at[span[0], :])

    @pl.when(is_one)
    def _():
        spread(1, two_hbm.at[:, span[0]], place(1, 0, my_col))
        spread(0, one_hbm.at[:, span[0]], place(0, 0, my_col))
        send_x(0, rest)

    @pl.when(is_zero)
    def _():
        send_x(0, rest)
        for block in range(1, blocks):
            send_z(0, block)

    @pl.when(lower)
    def _():
        for panel in range(2):
            send_x(panel, whole)
        for block in range(blocks):
            send_z(0, block)

    for load in loads[:3]:
        load.wait()
    local = lax.broadcasted_iota(jnp.int32, (width, width), 0)
    for block in range(blocks):
        hit = onehot(local, piv_two[...] - (block * process_rows + my_row) * width)
        picks[1, span[block], :] = hit.astype(BF16)
    sent_sel[...] = dot(panels[0, my_col], picks[1]).astype(BF16)

    def sel_copy():
        return remote(sent_sel, sel_in.at[my_row], s_send, s_recv, {"prow": 1})

    @pl.when(not_one)
    def _():
        sel_copy().start()

    for block in range(blocks):
        hit = onehot(local, piv_one[...] - (block * process_rows + my_row) * width)
        picks[0, span[block], :] = hit.astype(BF16)
    loads[3].wait()
    for which in range(2):
        rows_part[which] = dot_t(picks[which], matrix[...]).astype(BF16).reshape(2, half, cols)

    def top_copy():
        return remote(rows_part.at[1 - core], pair_rows, p_send, p_recv, {"prow": pair})

    def half_copy():
        return remote(rows_part.at[:, 1 - core], pair_rows, p_send, p_recv, {"prow": pair})

    def rows_copy(which):
        return remote(
            rows_part.at[which, core], group_rows.at[group, core], q_send, q_recv, {"prow": which}
        )

    def swap(which, rows):
        pick = picks[which]
        kept = 1.0 - jnp.sum(pick.astype(F32), axis=1, keepdims=True)
        matrix[...] = (matrix[...].astype(F32) * kept + dot(pick, rows)).astype(BF16)

    def update(panel, block, to):
        to[span[block], :] = (
            matrix[span[block], :].astype(F32) - dot_t(block_of(panel, block), solved[panel])
        ).astype(BF16)

    def chosen():
        total = rows_part[core].astype(F32) + pair_rows[...].astype(F32)
        arrived(group_rows.at[pl.ds(0, groups - 1)], q_recv)
        for source in range(1, groups):
            total = total + group_rows[source].astype(F32)
        return total.astype(BF16).reshape(width, cols)

    def solve(incoming):
        return (dot(inverse[0], incoming) + dot(inverse[1], incoming)).astype(BF16)

    @pl.when(top)
    def _():
        top_copy().start()

    @pl.when(is_zero)
    def _():
        send_x(1, rest)
        for block in range(1, blocks):
            send_z(1, block)
        lead[0] = matrix[span[0], :]
        swap(0, lead[0])

    @pl.when(is_one)
    def _():
        selected = sent_sel[...].astype(F32)
        arrived(sel_in.at[pl.ds(0, process_rows - 1)], s_recv)
        for step in range(1, process_rows):
            selected = selected + sel_in[row_peer(step)].astype(F32)
        chosen_panel[my_col] = selected.astype(BF16)
        spread(2, chosen_panel.at[my_col], chosen_panel.at[my_col])
        for block in range(1, blocks):
            send_z(0, block)
        send_x(1, rest)
        for block in range(1, blocks):
            send_z(1, block)
        spread_on(1)
        item_wait(LEAD_ONE)
        pick = picks[0, span[0], :]
        kept = 1.0 - jnp.sum(pick.astype(F32), axis=1, keepdims=True)
        lead[1] = (matrix[span[0], :].astype(F32) * kept + dot(pick, lead[0])).astype(BF16)
        item_down(LEAD_TWO)
        spread_on(0)
        swap(0, lead[0])

    @pl.when(top)
    def _():
        loads[4].wait()

    @pl.when(is_zero)
    def _():
        take_direct(0)

        def pause(step):
            if step == 4:
                forward_if(inside, 0, (1,))

        result = unit_inverse(block_of(0, 0), pause)
        inverse[0], inverse[1] = halves(result)
        top_copy().wait_recv()
        solved[0] = solve(chosen())
        item_across(SOLVED_ONE)
        item_down(SOLVED_ONE)
        forward_if(at_end, 0, (1,))
        for block in range(2, blocks):
            forward(0, block)

    @pl.when(is_one)
    def _():
        spread_on(2)
        take_spread(1)

        def pause(step):
            pass

        result = unit_inverse(block_of(1, 0), pause)
        inverse[0], inverse[1] = halves(result)
        first_across = jnp.broadcast_to(piv_one[...], (width, width))
        second_down = jnp.broadcast_to(piv_two[...].astype(F32), (width, width)).T.astype(jnp.int32)
        take_spread(0)
        cross[...] = panels[0, :, :, span[0]]
        item_down(CROSS)
        forward_if(inside, 0, range(1, blocks))
        match = onehot(second_down, first_across)
        kept = 1.0 - jnp.sum(match, axis=1, keepdims=True)
        top_copy().wait_recv()
        swapped = chosen().astype(F32) * kept + dot(match.astype(BF16), lead[0])
        take_spread(2)
        item_wait(SOLVED_ONE)
        incoming = (swapped - dot_t(chosen_panel[...].reshape(width, width), solved[0])).astype(BF16)
        solved[1] = solve(incoming)
        item_down(SOLVED_TWO)
        item_across(SOLVED_TWO)
        leaving[...] = (lead[1].astype(F32) - dot_t(block_of(0, 0), solved[0])).astype(BF16)
        item_across(LEAVING_TWO)
        forward_if(at_end, 0, range(1, blocks))

    @pl.when(top)
    def _():
        pass_beside(rest)
        for block in range(1, blocks):
            forward(1, block)
        take_x(0, rest)
        for block in range(1, blocks):
            take(0, block)
            update(0, block, matrix)

    @pl.when(is_zero)
    def _():
        item_wait(LEAVING_TWO)
        swap(1, leaving[...])
        item_wait(SOLVED_TWO)
        out[span[0], :] = solved[0]

    @pl.when(is_one)
    def _():
        swap(1, leaving[...])
        out[span[0], :] = solved[1]

    @pl.when(top)
    def _():
        take_beside(rest)
        for block in range(1, blocks):
            take(1, block)
            update(1, block, out)

    @pl.when(lower)
    def _():
        half_copy().start()
        for block in range(blocks):
            send_z(1, block)
        half_copy().wait_recv()
        for which in range(2):
            rows_part[which, core] = (
                rows_part[which, core].astype(F32) + pair_rows[which].astype(F32)
            ).astype(BF16)
            rows_copy(which).start()
        loads[4].wait()
        forward(0, 0)

    @pl.when(lower_zero)
    def _():
        item_relay(LEAD_ONE)

    @pl.when(lower_one)
    def _():
        item_wait(LEAD_ONE)

    @pl.when(lower)
    def _():
        swap(0, lead[0])
        forward(0, 1)
        pass_beside(whole)
        for block in range(2, blocks):
            forward(0, block)

    @pl.when(lower_one)
    def _():
        item_relay(LEAD_TWO)

    @pl.when(lower)
    def _():
        forward(1, 0)
        forward_if(inside, 1, range(1, blocks))
        forward_if(at_end, 1, (1,))

    @pl.when(lower_one)
    def _():
        item_relay(CROSS)

    @pl.when(lower_zero)
    def _():
        item_relay(SOLVED_ONE)

    @pl.when(lower)
    def _():
        forward_if(at_end, 1, range(2, blocks))

    @pl.when(lower_zero)
    def _():
        item_wait(LEAD_TWO)
        item_wait(CROSS)

    @pl.when(lower_one)
    def _():
        item_relay(SOLVED_TWO)
        item_wait(SOLVED_ONE)

    @pl.when(lower)
    def _():
        take_x(0, whole)
        for block in range(blocks):
            take(0, block)
            update(0, block, matrix)
        leaving[...] = (lead[1].astype(F32) - dot_t(cross[...].reshape(width, width), solved[0])).astype(BF16)
        swap(1, leaving[...])

    @pl.when(lower_zero)
    def _():
        item_wait(SOLVED_TWO)

    @pl.when(lower)
    def _():
        take_beside(whole)
        for block in range(blocks):
            take(1, block)
            update(1, block, out)
        all_departed(whole)
        half_copy().wait_send()
        departed(rows_part.at[:, core], q_send)

    @pl.when(lower_zero)
    def _():
        item_sent(LEAD_ONE, 1)
        item_sent(SOLVED_ONE, 1)

    @pl.when(lower_one)
    def _():
        item_sent(LEAD_TWO, 1)
        item_sent(CROSS, 1)
        item_sent(SOLVED_TWO, 1)

    @pl.when(top)
    def _():
        all_departed(rest)
        top_copy().wait_send()
        departed(others(), d_send.at[0])

    @pl.when(is_zero)
    def _():
        item_sent(LEAD_ONE, groups)
        item_sent(SOLVED_ONE, groups)

    @pl.when(is_one)
    def _():
        departed(others(), d_send.at[1])
        departed(others(), d_send.at[2])
        item_sent(LEAD_TWO, groups - 1)
        item_sent(CROSS, groups - 1)
        item_sent(SOLVED_TWO, groups)
        item_sent(LEAVING_TWO, 1)

    @pl.when(not_one)
    def _():
        sel_copy().wait_send()


def on_device(matrix, panel_one, panel_two, pivots_one, pivots_two):
    process_rows = lax.axis_size("prow")
    process_cols = lax.axis_size("pcol")
    shard, rows_dev = panel_one.shape
    width = pivots_one.shape[0]
    cols = matrix.shape[1]
    vmem = pl.BlockSpec(memory_space=pltpu.VMEM)
    hbm = pl.BlockSpec(memory_space=pltpu.HBM)
    dma = pltpu.SemaphoreType.DMA
    assert rows_dev > width and rows_dev % width == 0 and shard * process_cols == width
    assert process_cols % 4 == 0 and process_cols >= 8 and process_rows % 2 == 0
    groups = process_rows // 2
    blocks = rows_dev // width
    operands = (matrix, panel_one, panel_two, pivots_one.reshape(1, width), pivots_two.reshape(1, width))
    return pl.pallas_call(
        functools.partial(body, process_rows, process_cols),
        out_shape=jax.ShapeDtypeStruct(matrix.shape, BF16),
        in_specs=[hbm] * 5,
        out_specs=vmem,
        scratch_shapes=[
            pltpu.VMEM((1, width), jnp.int32),
            pltpu.VMEM((1, width), jnp.int32),
            pltpu.VMEM((rows_dev, cols), BF16),
            pltpu.VMEM((2, rows_dev, width), BF16),
            pltpu.VMEM((2, process_cols, shard, rows_dev), BF16),
            pltpu.VMEM((process_cols, shard, width), BF16),
            pltpu.VMEM((shard, width), BF16),
            pltpu.VMEM((process_rows, shard, width), BF16),
            pltpu.VMEM((2, 2, width // 2, cols), BF16),
            pltpu.VMEM((2, width // 2, cols), BF16),
            pltpu.VMEM((groups, 2, width // 2, cols), BF16),
            pltpu.VMEM((2, width, cols), BF16),
            pltpu.VMEM((process_cols, shard, width), BF16),
            pltpu.VMEM((2, width, cols), BF16),
            pltpu.VMEM((width, cols), BF16),
            pltpu.VMEM((2, width, width), BF16),
            dma((5,)),
            dma((2,)), dma((2, blocks)), dma((2, blocks)), dma((3,)),
            dma((3,)), dma((3,)), dma((3,)),
            dma, dma,
            dma, dma,
            dma, dma,
            dma((6,)), dma((6,)),
        ],
        compiler_params=pltpu.CompilerParams(
            collective_id=0, has_side_effects=True, vmem_limit_bytes=32 * 1024 * 1024
        ),
    )(*[pltpu.with_memory_space_constraint(operand, pltpu.HBM) for operand in operands])


def solution(mesh):
    placed = (P("prow", "pcol"), P("pcol", "prow"), P("pcol", "prow"), P(), P())
    return jax.shard_map(
        on_device, mesh=mesh, in_specs=placed, out_specs=P("prow", "pcol"), check_vma=False
    )
```
